512 devices in a mesh: adv: 8 (over y, core), imp: 64 (over z, x).
Axes of the slice: x: 4, y: 4, z: 16, core: 2. Of those that a mesh axis runs over, the one named last changes fastest.
Arguments:
- adv_embed: float32 [16384, 64], P(('adv', 'imp')), may hold values from -5 to 5
- imp_embed: float32 [32768, 64], P(('imp', 'adv')), may hold values from -5 to 5
- value_scale: float32 [16384], P('adv'), may hold values from 0.3 to 3
- spend_class: int32 [16384], P('adv'), may hold values from 0 to 7
- eligible: int32 [128, 256], P('adv', 'imp'), may hold values from 0 to 1, as said below
Outputs:
- bid_density: float32 [16384, 32768], P('adv', 'imp')
- prices: float32 [32768], P('imp')
- pacing: float32 [16384], P('adv')
The draws below stay inside these ranges and needn't reach their ends.
Inputs may be any that keep to these rules, and one draw needn't show every extreme that they name: Every impression block is eligible for at least one advertiser block.
All inputs are finite; a program needn't handle non-finite values.
Results may differ from the reference program's by a relative error of at most 0.0002.
Values sent between devices are 32-bit elements; how exact they have to be, the bound alone decides.
A program may use at most 64 MiB of HBM per device.

```python
import math
import jax
import jax.numpy as jnp
from jax import lax

EMB = 64
BLOCK = 128
ITERS = 2
ADV_DEV = 2048
ADVS = 16384
IMPS = 32768
N_ADV = 8


def draw_eligible(key, part):
    block_rows = ADVS // BLOCK
    block_cols = IMPS // BLOCK
    random_bits = jax.random.randint(key, (block_rows, block_cols), 0, 2, dtype=jnp.int32)
    row_index = jnp.arange(block_rows, dtype=jnp.int32)[:, None]
    col_index = jnp.arange(block_cols, dtype=jnp.int32)[None, :]
    forced = (row_index == col_index % block_rows).astype(jnp.int32)
    return jnp.maximum(random_bits, forced).astype(jnp.int32)


def with_ends(drawn, own_key, least, top_value):
    longest = drawn.shape.index(max(drawn.shape))
    spots = []
    for shift in (0, 1):
        where = [jax.random.randint(jax.random.fold_in(own_key, axis), (), 0, length) for axis, length in enumerate(drawn.shape)]
        where[longest] = (where[longest] + shift) % drawn.shape[longest]
        spots.append(tuple(where))
    return drawn.at[spots[0]].set(least).at[spots[1]].set(top_value)


def block_levels(key, shape, shards, low, high):
    def one(dim, blocks):
        steps = jax.random.uniform(jax.random.fold_in(jax.random.fold_in(key, 6), dim), (blocks,), jnp.float32, low / len(shards), high / len(shards))
        return jnp.repeat(jnp.exp(steps), shape[dim] // blocks).reshape((-1,) + (1,) * (len(shape) - dim - 1))

    level = one(*shards[0])
    for cut in shards[1:]:
        level = level * one(*cut)
    return level


def gaussian(key, extent, deviation, reach, split=(), held_as=jnp.bfloat16):
    entries = deviation * jax.random.normal(key, extent, jnp.float32)
    if split:
        entries = entries * block_levels(key, extent, split, -0.22, 0.18)
    return jnp.clip(entries, -reach, reach).astype(held_as)


def setup_inputs(seed: int = 0) -> dict:
    arg_keys = jax.random.split(jax.random.key(seed), 6)
    adv_embed = gaussian(arg_keys[0], (ADVS, EMB), 1.0, 5.0, ((0, 512),), jnp.float32)
    imp_embed = gaussian(arg_keys[1], (IMPS, EMB), 1.0, 5.0, ((0, 512),), jnp.float32)
    value_scale = jnp.clip(jnp.exp(math.log(3.0) - 2.3025851 * jax.random.uniform(arg_keys[2], (ADVS,), jnp.float32) ** block_levels(arg_keys[2], (ADVS,), ((0, 8),), -0.2, 0.2)), 0.3, 3.0)
    spend_class = with_ends(jax.random.randint(arg_keys[3], (ADVS,), 0, 8), jax.random.fold_in(arg_keys[3], 1), 0, 7).astype(jnp.int32)
    eligible = draw_eligible(jax.random.fold_in(arg_keys[5], 71), 0)
    return {"adv_embed": adv_embed, "imp_embed": imp_embed, "value_scale": value_scale, "spend_class": spend_class, "eligible": eligible}


score_gain = 0.0875


def block_values(embed_rows, scale_rows, mask_rows, imp_embed):
    scores = jnp.einsum("ae,ie->ai", embed_rows, imp_embed, precision=lax.Precision.HIGHEST, preferred_element_type=jnp.float32) * score_gain
    count_rows = mask_rows.shape[0]
    count_cols = mask_rows.shape[1]
    expanded = jnp.broadcast_to(mask_rows.astype(jnp.float32)[:, None, :, None], (count_rows, BLOCK, count_cols, BLOCK))
    blocks_mask = expanded.reshape(count_rows * BLOCK, count_cols * BLOCK)
    values = scale_rows[:, None] * jnp.exp(scores) * blocks_mask
    return values, blocks_mask


def block_bids(embed_rows, scale_rows, mask_rows, limit_rows, adv_factor, imp_factor, power, imp_embed):
    values, blocks_mask = block_values(embed_rows, scale_rows, mask_rows, imp_embed)
    bid_tile = blocks_mask * limit_rows[:, None] / IMPS
    for step in range(power):
        bid_tile = bid_tile * values
    bid_tile = bid_tile * adv_factor[:, None] / imp_factor[None, :]
    return values, bid_tile


def reference(adv_embed, imp_embed, value_scale, spend_class, eligible):
    allowance = (IMPS / ADVS) * jnp.exp(0.3 * spend_class.astype(jnp.float32) - 1.2)
    embed_groups = adv_embed.reshape(N_ADV, ADV_DEV, EMB)
    scale_groups = value_scale.reshape(N_ADV, ADV_DEV)
    limit_groups = allowance.reshape(N_ADV, ADV_DEV)
    mask_groups = eligible.reshape(N_ADV, ADV_DEV // BLOCK, IMPS // BLOCK)
    adv_factor = jnp.ones((N_ADV, ADV_DEV), jnp.float32)
    imp_factor = jnp.ones((IMPS,), jnp.float32)
    prices = jnp.ones((IMPS,), jnp.float32)
    pacing_groups = jnp.ones((N_ADV, ADV_DEV), jnp.float32)
    for power in range(ITERS):
        def column_sums(packed, power=power, imp_factor=imp_factor):
            values, bid_tile = block_bids(packed[0], packed[1], packed[2], packed[3], packed[4], imp_factor, power, imp_embed)
            return jnp.sum(bid_tile, axis=0)

        prices = jnp.sum(lax.map(column_sums, (embed_groups, scale_groups, mask_groups, limit_groups, adv_factor)), axis=0)

        def row_sums(packed, power=power, imp_factor=imp_factor, prices=prices):
            values, bid_tile = block_bids(packed[0], packed[1], packed[2], packed[3], packed[4], imp_factor, power, imp_embed)
            gain = values * bid_tile / prices[None, :]
            return jnp.sum(gain, axis=1)

        spending = lax.map(row_sums, (embed_groups, scale_groups, mask_groups, limit_groups, adv_factor))
        pacing_groups = limit_groups / jnp.maximum(spending, limit_groups)
        adv_factor = adv_factor * pacing_groups
        imp_factor = imp_factor * prices

    def final_bids(packed):
        values, bid_tile = block_bids(packed[0], packed[1], packed[2], packed[3], packed[4], imp_factor, ITERS, imp_embed)
        return bid_tile * ADVS

    density = lax.map(final_bids, (embed_groups, scale_groups, mask_groups, limit_groups, adv_factor))
    return density.reshape(ADVS, IMPS), prices, pacing_groups.reshape(ADVS)
```

```python
import functools

import jax
import jax.numpy as jnp
from jax import lax
from jax.experimental import pallas as pl
from jax.experimental.pallas import tpu as pltpu
from jax.sharding import PartitionSpec as P

MESH = pl.DeviceIdType.MESH
BLOCK = 128
SCORE_GAIN = 0.0875
LOG2E = 1.4426950408889634
NX = 4
NZ = 16
NA = 8
F32 = jnp.float32
BF16 = jnp.bfloat16

NEAR = (1, -1, 2, -2, 3, -3, 4, -4)
FAR_NEG = (1, 2, 3, 4)
FAR_POS = (1, 2, 3)
WINDOW = (1, -1, 2, -2)
JUMP = (5, -5)
ALL_D = (0, 1, -1, 2, -2, 3, -3, 4, -4, 5, -5, 6, -6, 7, -7, 8)

_n = 0
S_Z = {}
for _d in ALL_D[1:]:
    S_Z[_d] = _n
    _n += 1
S_X = {}
for _d in ALL_D:
    for _e in (1, 2, 3):
        S_X[_d, _e] = _n
        _n += 1
S_IMP = {}
S_P1 = {}
S_P2 = {}
for _k in range(1, NA):
    S_IMP[_k] = _n
    S_P1[_k] = _n + 1
    S_P2[_k] = _n + 2
    _n += 3
S_RX = {}
S_RZ = {}
for _round in range(2):
    for _e in (1, 2, 3):
        S_RX[_round, _e] = _n
        _n += 1
    for _d in WINDOW + JUMP + (8,):
        S_RZ[_round, _d] = _n
        _n += 1
N_SEM = _n


def split_parts(rows):
    high = rows.astype(BF16).astype(F32)
    rest = rows - high
    mid = rest.astype(BF16).astype(F32)
    low = rest - mid
    return high, mid, low


def first_half(shape):
    return lax.broadcasted_iota(jnp.int32, shape, len(shape) - 1) < 64


def twice(packed):
    turned = pltpu.roll(packed, 64, axis=len(packed.shape) - 1)
    left = first_half(packed.shape)
    return jnp.where(left, packed, turned), jnp.where(left, turned, packed)


def exchange_kernel(
    adv_hbm,
    imp_hbm,
    scale_hbm,
    class_hbm,
    elig_hbm,
    a_out,
    b_out,
    aux_out,
    adv_in,
    imp_in,
    scale_ref,
    class_ref,
    elig_ref,
    adv_buf,
    imp_buf,
    a_ref,
    b_ref,
    e_ref,
    t_ref,
    p1_buf,
    p2_buf,
    r1_ref,
    c2_ref,
    sums,
    rx_buf,
    rz_buf,
    aux_ref,
    send_sem,
    recv_sem,
    in_sem,
    out_sem,
):
    adv = lax.axis_index("adv")
    imp = lax.axis_index("imp")
    z = imp // NX
    x = lax.rem(imp, NX)

    def at_z(d):
        return lax.rem(z + (d + NZ), NZ)

    def at_x(e):
        return lax.rem(x + e, NX)

    def slot(d, e):
        return at_z(d) * NX + at_x(e)

    def to_z(d):
        return (adv, at_z(d) * NX + x)

    def to_x(e):
        return (adv, z * NX + at_x(e))

    def to_adv(k):
        return (lax.rem(adv + k, NA), imp)

    started = []

    def remote(src, dst, number, device):
        return pltpu.make_async_remote_copy(
            src_ref=src,
            dst_ref=dst,
            send_sem=send_sem.at[number],
            recv_sem=recv_sem.at[number],
            device_id=device,
            device_id_type=MESH,
        )

    def send(src, dst, number, device):
        copy = remote(src, dst, number, device)
        copy.start()
        started.append(copy)

    def arrived(ref, number):
        remote(ref, ref, number, to_x(1)).wait_recv()

    barrier = pltpu.get_barrier_semaphore()
    peers = [to_z(d) for d in NEAR] + [to_x(e) for e in (1, 2, 3)] + [to_adv(k) for k in range(1, NA)]
    for device in peers:
        pl.semaphore_signal(barrier, inc=1, device_id=device, device_id_type=MESH)

    loads = [
        pltpu.make_async_copy(src, dst, in_sem.at[n])
        for n, (src, dst) in enumerate(
            (
                (adv_hbm, adv_in),
                (imp_hbm, imp_in),
                (scale_hbm, scale_ref),
                (class_hbm, class_ref),
                (elig_hbm, elig_ref),
            )
        )
    ]
    for load in loads:
        load.start()
    for load in loads:
        load.wait()

    mine = slot(0, 0)
    adv_buf[mine] = jnp.concatenate([adv_in[0:16, :], adv_in[16:32, :]], axis=1)
    imp_buf[adv] = jnp.concatenate([imp_in[0:32, :], imp_in[32:64, :]], axis=1)
    allowance = 2.0 * jnp.exp(0.3 * class_ref[...].astype(F32) - 1.2)
    mask = elig_ref[...].astype(F32)
    p1_buf[adv] = jnp.zeros((8, BLOCK), F32)
    for cb in range(4):
        p1_buf[adv, cb : cb + 1, :] = jnp.sum(allowance * mask[:, cb : cb + 1], axis=0, keepdims=True)

    pl.semaphore_wait(barrier, len(peers))

    for d in (4, -4, 3, -3, 2, -2, 1, -1):
        send(adv_buf.at[mine], adv_buf.at[mine], S_Z[-d], to_z(d))
    for k in range(1, NA):
        send(imp_buf.at[adv], imp_buf.at[adv], S_IMP[k], to_adv(k))
    for e in (2, 1, 3):
        send(adv_buf.at[mine], adv_buf.at[mine], S_X[0, e], to_x(e))
    for k in range(1, NA):
        send(p1_buf.at[adv], p1_buf.at[adv], S_P1[k], to_adv(k))

    def pass_on(d):
        here = adv_buf.at[slot(d, 0)]
        arrived(here, S_Z[d])
        if d == -4:
            for k in FAR_NEG:
                far = -4 - k
                send(here, here, S_Z[8 if far == -8 else far], to_z(k))
        if d == 4:
            for k in FAR_POS:
                send(here, here, S_Z[4 + k], to_z(-k))
        for e in (2, 1, 3):
            send(here, here, S_X[d, e], to_x(e))

    for d in NEAR:
        pass_on(d)

    for k in range(1, NA):
        arrived(p1_buf.at[lax.rem(adv + (NA - k), NA)], S_P1[k])
    share = p1_buf[0]
    for k in range(1, NA):
        share = share + p1_buf[k]
    first_price = jnp.sum(share, axis=1, keepdims=True) / 32768.0
    weights = [mask[:, cb : cb + 1] / first_price[cb : cb + 1, :] for cb in range(4)]

    for k in range(1, NA):
        arrived(imp_buf.at[lax.rem(adv + (NA - k), NA)], S_IMP[k])
    low_half, up_half = twice(imp_buf[...] * (SCORE_GAIN * LOG2E))
    doubled = jnp.concatenate([low_half, up_half], axis=1).reshape(512, BLOCK)
    high, mid, low = split_parts(doubled)
    left = first_half((512, BLOCK))
    b_ref[:, 0:128] = jnp.where(left, high, mid).astype(BF16)
    b_ref[:, 128:256] = jnp.where(left, high, low).astype(BF16)
    b_ref[:, 256:384] = jnp.where(left, mid, high).astype(BF16)

    def chunk(d):
        p = lax.rem(z // 2 + (d + 8), 8)
        low_half, up_half = twice(adv_buf[pl.ds(p * 8, 8)])
        doubled = jnp.concatenate([low_half, up_half], axis=1).reshape(256, BLOCK)
        high, mid, low = split_parts(doubled)
        left = first_half((256, BLOCK))
        a_ref[p, :, 0:128] = high.astype(BF16)
        a_ref[p, :, 128:256] = jnp.where(left, mid, high).astype(BF16)
        a_ref[p, :, 256:384] = jnp.where(left, mid, low).astype(BF16)
        rows = a_ref[p]

        @pl.loop(0, 4)
        def _(cb):
            start = pl.multiple_of(cb * BLOCK, BLOCK)
            scores = lax.dot_general(
                b_ref[pl.ds(start, BLOCK), :],
                rows,
                (((1,), (1,)), ((), ())),
                preferred_element_type=F32,
            )
            values = jnp.exp2(scores)
            e_ref[p, cb] = values
            total = jnp.sum(values, axis=0, keepdims=True)
            t_ref[cb, pl.ds(p * 2, 1), :] = total[:, 0:128]
            t_ref[cb, pl.ds(p * 2 + 1, 1), :] = total[:, 128:256]

    def from_x(d):
        for e in (1, 2, 3):
            arrived(adv_buf.at[slot(d, NX - e)], S_X[d, e])

    for d in (0, 1, -1):
        from_x(d)
    chunk(0)
    for d in (2, -2, 3, -3):
        from_x(d)
    chunk(1)
    chunk(-1)
    for d in (5, -5, 6, -6, 7, -7, 8):
        pass_on(d)
    for d in (4, -4, 5, -5):
        from_x(d)
    chunk(2)
    chunk(-2)
    for d in (6, -6, 7, -7, 8):
        from_x(d)
    chunk(3)
    chunk(-3)
    chunk(4)

    keep = [
        pltpu.make_async_copy(a_ref, a_out, out_sem.at[0]),
        pltpu.make_async_copy(b_ref, b_out, out_sem.at[1]),
    ]
    for copy in keep:
        copy.start()

    def sum_over_imp(n, part):
        sums[n, 0] = part
        for e in (2, 1, 3):
            send(sums.at[n, 0], rx_buf.at[n, e - 1], S_RX[n, e], to_x(e))
        got = {0: part}
        for e in (1, 3, 2):
            arrived(rx_buf.at[n, e - 1], S_RX[n, e])
        total = part + rx_buf[n, 1] + (rx_buf[n, 0] + rx_buf[n, 2])
        sums[n, 1] = total
        index = {d: i for i, d in enumerate(WINDOW + JUMP + (8,))}

        def shift(which, d):
            send(sums.at[n, which], rz_buf.at[n, index[d]], S_RZ[n, d], to_z(-d))

        for d in (2, -2, 1, -1, 8):
            shift(1, d)
        for d in WINDOW:
            arrived(rz_buf.at[n, index[d]], S_RZ[n, d])
        window = total + ((rz_buf[n, 0] + rz_buf[n, 1]) + (rz_buf[n, 2] + rz_buf[n, 3]))
        sums[n, 2] = window
        for d in JUMP:
            shift(2, d)
        for d in JUMP + (8,):
            arrived(rz_buf.at[n, index[d]], S_RZ[n, d])
        return window + (rz_buf[n, 4] + rz_buf[n, 5]) + rz_buf[n, 6]

    scale = scale_ref[...]
    first_bid = allowance * scale / 32768.0
    part = t_ref[0] * weights[0]
    for cb in range(1, 4):
        part = part + t_ref[cb] * weights[cb]
    spending = sum_over_imp(0, part) * first_bid
    pacing = allowance / jnp.maximum(spending, allowance)
    row_bid = first_bid * pacing
    for cb in range(4):
        r1_ref[cb] = row_bid * weights[cb]

    mine_p2 = p2_buf.at[adv]
    p2_buf[adv] = jnp.ones((8, BLOCK), F32)

    @pl.loop(0, 4)
    def _(cb):
        total = jnp.zeros((BLOCK, BLOCK), F32)
        for p in range(8):
            for half in range(2):
                row = r1_ref[cb, pl.ds(2 * p + half, 1), :]
                total = total + e_ref[p, cb, :, half * 128 : half * 128 + 128] * row
        p2_buf[adv, pl.ds(cb, 1), :] = jnp.sum(total.T, axis=0, keepdims=True)

    for k in range(1, NA):
        send(mine_p2, mine_p2, S_P2[k], to_adv(k))
    for k in range(1, NA):
        arrived(p2_buf.at[lax.rem(adv + (NA - k), NA)], S_P2[k])
    price = p2_buf[0]
    for k in range(1, NA):
        price = price + p2_buf[k]
    inverse = 1.0 / price
    for cb in range(4):
        c2_ref[cb] = jnp.broadcast_to(inverse[cb : cb + 1, :], (BLOCK, BLOCK)).T

    @pl.loop(0, 8)
    def _(p):
        for half in range(2):
            total = jnp.zeros((8, BLOCK), F32)
            for cb in range(4):
                row = r1_ref[cb, pl.ds(2 * p + half, 1), :]
                value = e_ref[p, cb, :, half * 128 : half * 128 + 128]
                gain = (value * row) * c2_ref[cb] * value
                total = total + jnp.sum(gain.reshape(16, 8, BLOCK), axis=0)
            t_ref[0, pl.ds(2 * p + half, 1), :] = jnp.sum(total, axis=0, keepdims=True)

    spending = sum_over_imp(1, t_ref[0]) * scale
    pacing = allowance / jnp.maximum(spending, allowance)
    aux_ref[0:16] = row_bid
    aux_ref[16:32] = scale * pacing * 16384.0
    aux_ref[32:48] = pacing
    aux_ref[48:56] = price
    for cb in range(4):
        aux_ref[56 + 16 * cb : 72 + 16 * cb] = jnp.broadcast_to(weights[cb], (16, BLOCK))
    last = pltpu.make_async_copy(aux_ref, aux_out, out_sem.at[2])
    last.start()
    for copy in keep:
        copy.wait()
    for copy in started:
        copy.wait_send()
    last.wait()


def tile_kernel(a_ref, b_ref, aux_ref, out_ref, price_ref, pacing_ref):
    step = pl.program_id(0)
    price = aux_ref[48:52, :]
    price_ref[...] = price
    pacing_ref[...] = aux_ref[32:48, :]
    inverse = 1.0 / price
    for half in range(2):
        rb = step * 2 + half

        def column(start):
            row = aux_ref[pl.ds(start + rb, 1), :]
            return jnp.broadcast_to(row, (BLOCK, BLOCK)).T

        first = column(0)
        second = column(16)
        for cb in range(4):
            scores = lax.dot_general(
                a_ref[half * 128 : half * 128 + 128, :],
                b_ref[cb * 128 : cb * 128 + 128, :],
                (((1,), (1,)), ((), ())),
                preferred_element_type=F32,
            )
            value = jnp.exp2(scores)
            weight = aux_ref[pl.ds(56 + 16 * cb + rb, 1), :]
            bid = value * (first * weight)
            out_ref[half * 128 : half * 128 + 128, cb * 128 : cb * 128 + 128] = (
                bid * inverse[cb : cb + 1, :] * value * second
            )


def per_device(adv_embed, imp_embed, value_scale, spend_class, eligible):
    hbm = pl.BlockSpec(memory_space=pl.ANY)
    a_pack, b_pack, aux = pl.pallas_call(
        exchange_kernel,
        out_shape=(
            jax.ShapeDtypeStruct((8, 256, 384), BF16),
            jax.ShapeDtypeStruct((512, 384), BF16),
            jax.ShapeDtypeStruct((120, BLOCK), F32),
        ),
        in_specs=[hbm] * 5,
        out_specs=[hbm] * 3,
        scratch_shapes=[
            pltpu.VMEM((32, 64), F32),
            pltpu.VMEM((64, 64), F32),
            pltpu.VMEM((16, BLOCK), F32),
            pltpu.VMEM((16, BLOCK), jnp.int32),
            pltpu.VMEM((16, 4), jnp.int32),
            pltpu.VMEM((64, 16, BLOCK), F32),
            pltpu.VMEM((8, 32, BLOCK), F32),
            pltpu.VMEM((8, 256, 384), BF16),
            pltpu.VMEM((512, 384), BF16),
            pltpu.VMEM((8, 4, BLOCK, 256), F32),
            pltpu.VMEM((4, 16, BLOCK), F32),
            pltpu.VMEM((NA, 8, BLOCK), F32),
            pltpu.VMEM((NA, 8, BLOCK), F32),
            pltpu.VMEM((4, 16, BLOCK), F32),
            pltpu.VMEM((4, BLOCK, BLOCK), F32),
            pltpu.VMEM((2, 3, 16, BLOCK), F32),
            pltpu.VMEM((2, 3, 16, BLOCK), F32),
            pltpu.VMEM((2, 7, 16, BLOCK), F32),
            pltpu.VMEM((120, BLOCK), F32),
            pltpu.SemaphoreType.DMA((N_SEM,)),
            pltpu.SemaphoreType.DMA((N_SEM,)),
            pltpu.SemaphoreType.DMA((5,)),
            pltpu.SemaphoreType.DMA((3,)),
        ],
        compiler_params=pltpu.CompilerParams(
            collective_id=0, has_side_effects=True, vmem_limit_bytes=32 * 1024 * 1024
        ),
        name="exchange",
    )(
        adv_embed,
        imp_embed,
        value_scale.reshape(16, BLOCK),
        spend_class.reshape(16, BLOCK),
        eligible,
    )
    density, prices, pacing = pl.pallas_call(
        tile_kernel,
        grid=(8,),
        out_shape=(
            jax.ShapeDtypeStruct((2048, 512), F32),
            jax.ShapeDtypeStruct((4, BLOCK), F32),
            jax.ShapeDtypeStruct((16, BLOCK), F32),
        ),
        in_specs=[
            pl.BlockSpec((256, 384), lambda i: (i, 0)),
            pl.BlockSpec((512, 384), lambda i: (0, 0)),
            pl.BlockSpec((120, BLOCK), lambda i: (0, 0)),
        ],
        out_specs=[
            pl.BlockSpec((256, 512), lambda i: (i, 0)),
            pl.BlockSpec((4, BLOCK), lambda i: (0, 0)),
            pl.BlockSpec((16, BLOCK), lambda i: (0, 0)),
        ],
        name="tile",
    )(a_pack.reshape(2048, 384), b_pack, aux)
    return density, prices.reshape(512), pacing.reshape(2048)


def solution(mesh):
    in_specs = (
        P(("adv", "imp"), None),
        P(("imp", "adv"), None),
        P("adv"),
        P("adv"),
        P("adv", "imp"),
    )
    out_specs = (P("adv", "imp"), P("imp"), P("adv"))
    return jax.shard_map(
        per_device, mesh=mesh, in_specs=in_specs, out_specs=out_specs, check_vma=False
    )
```

```python
import functools

import jax
import jax.numpy as jnp
from jax import lax
from jax.experimental import pallas as pl
from jax.experimental.pallas import tpu as pltpu
from jax.sharding import PartitionSpec as P

MESH = pl.DeviceIdType.MESH
BLOCK = 128
SCORE_GAIN = 0.0875
LOG2E = 1.4426950408889634
NX = 4
NZ = 16
NA = 8
F32 = jnp.float32
BF16 = jnp.bfloat16

NEAR = (1, -1, 2, -2, 3, -3, 4, -4)
FAR_NEG = (1, 2, 3, 4)
FAR_POS = (1, 2, 3)
WINDOW = (1, -1, 2, -2)
JUMP = (5, -5)
ALL_D = (0, 1, -1, 2, -2, 3, -3, 4, -4, 5, -5, 6, -6, 7, -7, 8)

_n = 0
S_Z = {}
for _d in ALL_D[1:]:
    S_Z[_d] = _n
    _n += 1
S_X = {}
for _d in ALL_D:
    for _e in (1, 2, 3):
        S_X[_d, _e] = _n
        _n += 1
S_IMP = {}
S_P1 = {}
S_P2 = {}
for _k in range(1, NA):
    S_IMP[_k] = _n
    S_P1[_k] = _n + 1
    S_P2[_k] = _n + 2
    _n += 3
S_RX = {}
S_RZ = {}
for _round in range(2):
    for _e in (1, 2, 3):
        S_RX[_round, _e] = _n
        _n += 1
    for _d in WINDOW + JUMP + (8,):
        S_RZ[_round, _d] = _n
        _n += 1
N_SEM = _n


def split_parts(rows):
    high = rows.astype(BF16).astype(F32)
    rest = rows - high
    mid = rest.astype(BF16).astype(F32)
    low = rest - mid
    return high, mid, low


def first_half(shape):
    return lax.broadcasted_iota(jnp.int32, shape, len(shape) - 1) < 64


def twice(packed):
    turned = pltpu.roll(packed, 64, axis=len(packed.shape) - 1)
    left = first_half(packed.shape)
    return jnp.where(left, packed, turned), jnp.where(left, turned, packed)


def exchange_kernel(
    adv_hbm,
    imp_hbm,
    scale_hbm,
    class_hbm,
    elig_hbm,
    g_ref,
    aux_ref,
    adv_in,
    imp_in,
    scale_ref,
    class_ref,
    elig_ref,
    adv_buf,
    imp_buf,
    a_ref,
    b_ref,
    e_ref,
    t_ref,
    p1_buf,
    p2_buf,
    r1_ref,
    c2_ref,
    sums,
    rx_buf,
    rz_buf,
    w_ref,
    send_sem,
    recv_sem,
    in_sem,
):
    adv = lax.axis_index("adv")
    imp = lax.axis_index("imp")
    z = imp // NX
    x = lax.rem(imp, NX)

    def at_z(d):
        return lax.rem(z + (d + NZ), NZ)

    def at_x(e):
        return lax.rem(x + e, NX)

    def slot(d, e):
        return at_z(d) * NX + at_x(e)

    def to_z(d):
        return (adv, at_z(d) * NX + x)

    def to_x(e):
        return (adv, z * NX + at_x(e))

    def to_adv(k):
        return (lax.rem(adv + k, NA), imp)

    started = []

    def remote(src, dst, number, device):
        return pltpu.make_async_remote_copy(
            src_ref=src,
            dst_ref=dst,
            send_sem=send_sem.at[number],
            recv_sem=recv_sem.at[number],
            device_id=device,
            device_id_type=MESH,
        )

    def send(src, dst, number, device):
        copy = remote(src, dst, number, device)
        copy.start()
        started.append(copy)

    def arrived(ref, number):
        remote(ref, ref, number, to_x(1)).wait_recv()

    loads = [
        pltpu.make_async_copy(src, dst, in_sem.at[n])
        for n, (src, dst) in enumerate(
            (
                (adv_hbm, adv_in),
                (imp_hbm, imp_in),
                (scale_hbm, scale_ref),
                (class_hbm, class_ref),
                (elig_hbm, elig_ref),
            )
        )
    ]
    for load in loads:
        load.start()

    barrier = pltpu.get_barrier_semaphore()
    peers = [to_z(d) for d in NEAR] + [to_x(e) for e in (1, 2, 3)] + [to_adv(k) for k in range(1, NA)]
    for device in peers:
        pl.semaphore_signal(barrier, inc=1, device_id=device, device_id_type=MESH)

    mine = slot(0, 0)
    loads[0].wait()
    adv_buf[mine] = jnp.concatenate([adv_in[0:16, :], adv_in[16:32, :]], axis=1)
    loads[1].wait()
    imp_buf[adv] = jnp.concatenate([imp_in[0:32, :], imp_in[32:64, :]], axis=1)
    for load in loads[2:]:
        load.wait()
    allowance = 2.0 * jnp.exp(0.3 * class_ref[...].astype(F32) - 1.2)
    mask = elig_ref[...].astype(F32).T
    p1_buf[adv] = jnp.zeros((8, BLOCK), F32)
    for cb in range(4):
        p1_buf[adv, cb : cb + 1, :] = jnp.sum(allowance * mask[:, cb : cb + 1], axis=0, keepdims=True)

    pl.semaphore_wait(barrier, len(peers))

    for d in (4, -4, 3, -3, 2, -2, 1, -1):
        send(adv_buf.at[mine], adv_buf.at[mine], S_Z[-d], to_z(d))
    for k in range(1, NA):
        send(imp_buf.at[adv], imp_buf.at[adv], S_IMP[k], to_adv(k))
    for e in (2, 1, 3):
        send(adv_buf.at[mine], adv_buf.at[mine], S_X[0, e], to_x(e))
    for k in range(1, NA):
        send(p1_buf.at[adv], p1_buf.at[adv], S_P1[k], to_adv(k))

    def pass_on(d):
        here = adv_buf.at[slot(d, 0)]
        arrived(here, S_Z[d])
        if d == -4:
            for k in FAR_NEG:
                far = -4 - k
                send(here, here, S_Z[8 if far == -8 else far], to_z(k))
        if d == 4:
            for k in FAR_POS:
                send(here, here, S_Z[4 + k], to_z(-k))
        for e in (2, 1, 3):
            send(here, here, S_X[d, e], to_x(e))

    for d in NEAR:
        pass_on(d)

    for k in range(1, NA):
        arrived(p1_buf.at[lax.rem(adv + (NA - k), NA)], S_P1[k])
    share = p1_buf[0]
    for k in range(1, NA):
        share = share + p1_buf[k]
    first_price = jnp.sum(share, axis=1, keepdims=True) / 32768.0
    weights = [mask[:, cb : cb + 1] / first_price[cb : cb + 1, :] for cb in range(4)]
    for cb in range(4):
        w_ref[cb] = jnp.broadcast_to(weights[cb], (16, BLOCK))

    for k in range(1, NA):
        arrived(imp_buf.at[lax.rem(adv + (NA - k), NA)], S_IMP[k])
    low_half, up_half = twice(imp_buf[...] * (SCORE_GAIN * LOG2E))
    doubled = jnp.concatenate([low_half, up_half], axis=1).reshape(512, BLOCK)
    high, mid, low = split_parts(doubled)
    left = first_half((512, BLOCK))
    b_ref[:, 0:128] = jnp.where(left, high, mid).astype(BF16)
    b_ref[:, 128:256] = jnp.where(left, high, low).astype(BF16)
    b_ref[:, 256:384] = jnp.where(left, mid, high).astype(BF16)

    for d in (5, -5, 6, -6, 7, -7, 8):
        pass_on(d)

    def chunk(p):
        low_half, up_half = twice(adv_buf[pl.ds(p * 8, 8)])
        doubled = jnp.concatenate([low_half, up_half], axis=1).reshape(256, BLOCK)
        high, mid, low = split_parts(doubled)
        left = first_half((256, BLOCK))
        rows = jnp.concatenate(
            [
                high.astype(BF16),
                jnp.where(left, mid, high).astype(BF16),
                jnp.where(left, mid, low).astype(BF16),
            ],
            axis=1,
        )
        a_ref[p] = rows
        for cb in range(4):
            scores = lax.dot_general(
                b_ref[cb * BLOCK : cb * BLOCK + BLOCK, :],
                rows,
                (((1,), (1,)), ((), ())),
                preferred_element_type=F32,
            )
            values = jnp.exp2(scores)
            e_ref[p, cb] = values
            total = jnp.sum(values, axis=0, keepdims=True)
            t_ref[cb, pl.ds(p * 2, 1), :] = total[:, 0:128]
            t_ref[cb, pl.ds(p * 2 + 1, 1), :] = total[:, 128:256]

    def from_x(d):
        for e in (1, 2, 3):
            arrived(adv_buf.at[slot(d, NX - e)], S_X[d, e])

    half_z = z // 2

    def chunks(first, count):
        @pl.loop(0, count)
        def _(n):
            far = first + n // 2
            chunk(lax.rem(half_z + jnp.where(lax.rem(n, 2) == 0, far, 8 - far), 8))

    for d in (0, 1, -1):
        from_x(d)
    chunks(0, 1)
    for d in (2, -2, 3, -3, 4, -4, 5, -5):
        from_x(d)
    chunks(1, 4)
    for d in (6, -6, 7, -7, 8):
        from_x(d)
    chunks(3, 3)

    def sum_over_imp(n, part, work):
        sums[n, 0] = part
        for e in (2, 1, 3):
            send(sums.at[n, 0], rx_buf.at[n, e - 1], S_RX[n, e], to_x(e))
        work(0, 2)
        for e in (1, 3, 2):
            arrived(rx_buf.at[n, e - 1], S_RX[n, e])
        total = part + rx_buf[n, 1] + (rx_buf[n, 0] + rx_buf[n, 2])
        sums[n, 1] = total
        index = {d: i for i, d in enumerate(WINDOW + JUMP + (8,))}

        def shift(which, d):
            send(sums.at[n, which], rz_buf.at[n, index[d]], S_RZ[n, d], to_z(-d))

        for d in (2, -2, 1, -1, 8):
            shift(1, d)
        work(2, 4)
        for d in WINDOW:
            arrived(rz_buf.at[n, index[d]], S_RZ[n, d])
        window = total + ((rz_buf[n, 0] + rz_buf[n, 1]) + (rz_buf[n, 2] + rz_buf[n, 3]))
        sums[n, 2] = window
        for d in JUMP:
            shift(2, d)
        work(4, 8)
        for d in JUMP + (8,):
            arrived(rz_buf.at[n, index[d]], S_RZ[n, d])
        return window + (rz_buf[n, 4] + rz_buf[n, 5]) + rz_buf[n, 6]

    def tile_values(start, stop):
        @pl.loop(start, stop)
        def _(p):
            scores = lax.dot_general(
                a_ref[p], b_ref[...], (((1,), (1,)), ((), ())), preferred_element_type=F32
            )
            g_ref[pl.ds(pl.multiple_of(p * 256, 256), 256), :] = jnp.exp2(scores)

    scale = scale_ref[...]
    first_bid = allowance * scale / 32768.0
    part = t_ref[0] * w_ref[0]
    for cb in range(1, 4):
        part = part + t_ref[cb] * w_ref[cb]
    spending = sum_over_imp(0, part, tile_values) * first_bid
    pacing = allowance / jnp.maximum(spending, allowance)
    row_bid = first_bid * pacing
    for cb in range(4):
        r1_ref[cb] = row_bid * w_ref[cb]
    r1_ref[4] = row_bid

    mine_p2 = p2_buf.at[adv]
    p2_buf[adv] = jnp.ones((8, BLOCK), F32)
    for cb in range(4):
        total = None
        for rb in range(16):
            row = r1_ref[cb, rb : rb + 1, :]
            half = rb % 2
            term = e_ref[rb // 2, cb, :, half * 128 : half * 128 + 128] * row
            total = term if total is None else total + term
        p2_buf[adv, cb : cb + 1, :] = jnp.sum(total.T, axis=0, keepdims=True)

    for k in range(1, NA):
        send(mine_p2, mine_p2, S_P2[k], to_adv(k))

    @pl.loop(0, 8)
    def _(p):
        for half in range(2):
            for cb in range(4):
                row = r1_ref[cb, pl.ds(2 * p + half, 1), :]
                value = e_ref[p, cb, :, half * 128 : half * 128 + 128]
                e_ref[p, cb, :, half * 128 : half * 128 + 128] = (value * row) * value

    for k in range(1, NA):
        arrived(p2_buf.at[lax.rem(adv + (NA - k), NA)], S_P2[k])
    price = p2_buf[0]
    for k in range(1, NA):
        price = price + p2_buf[k]
    inverse = 1.0 / price
    for cb in range(4):
        c2_ref[cb] = jnp.broadcast_to(inverse[cb : cb + 1, :], (BLOCK, BLOCK)).T

    @pl.loop(0, 8)
    def _(p):
        for half in range(2):
            total = jnp.zeros((8, BLOCK), F32)
            for cb in range(4):
                gain = e_ref[p, cb, :, half * 128 : half * 128 + 128] * c2_ref[cb]
                total = total + jnp.sum(gain.reshape(16, 8, BLOCK), axis=0)
            t_ref[0, pl.ds(2 * p + half, 1), :] = jnp.sum(total, axis=0, keepdims=True)

    def tile_gains(start, stop):
        @pl.loop(start, stop)
        def _(p):
            for half in range(2):
                rb = 2 * p + half
                rows = pl.ds(pl.multiple_of(p * 256 + half * 128, 128), 128)
                first = jnp.broadcast_to(r1_ref[4, pl.ds(rb, 1), :], (BLOCK, BLOCK)).T
                for cb in range(4):
                    value = g_ref[rows, cb * 128 : cb * 128 + 128]
                    bid = value * (first * w_ref[cb, pl.ds(rb, 1), :])
                    g_ref[rows, cb * 128 : cb * 128 + 128] = bid * inverse[cb : cb + 1, :] * value

    spending = sum_over_imp(1, t_ref[0], tile_gains) * scale
    pacing = allowance / jnp.maximum(spending, allowance)
    aux_ref[0:16] = scale * pacing * 16384.0
    aux_ref[16:32] = pacing
    aux_ref[32:40] = price
    for copy in started:
        copy.wait_send()


def scale_kernel(g_ref, aux_ref, out_hbm, price_hbm, pacing_hbm, out_ref, sem):
    small = [
        pltpu.make_async_copy(aux_ref.at[32:36], price_hbm, sem.at[8]),
        pltpu.make_async_copy(aux_ref.at[16:32], pacing_hbm, sem.at[9]),
    ]
    copies = []
    for p in range(8):
        for half in range(2):
            rb = 2 * p + half
            column = jnp.broadcast_to(aux_ref[rb : rb + 1, :], (BLOCK, BLOCK)).T
            rows = slice(rb * 128, rb * 128 + 128)
            for cb in range(4):
                columns = slice(cb * 128, cb * 128 + 128)
                out_ref[rows, columns] = g_ref[rows, columns] * column
        span = slice(p * 256, p * 256 + 256)
        copies.append(pltpu.make_async_copy(out_ref.at[span], out_hbm.at[span], sem.at[p]))
        copies[-1].start()
    for copy in small:
        copy.start()
    for copy in copies + small:
        copy.wait()


def per_device(adv_embed, imp_embed, value_scale, spend_class, eligible):
    hbm = pl.BlockSpec(memory_space=pltpu.HBM)
    vmem = pl.BlockSpec(memory_space=pltpu.VMEM)
    gains, aux = pl.pallas_call(
        exchange_kernel,
        out_shape=(
            jax.ShapeDtypeStruct((2048, 512), F32),
            jax.ShapeDtypeStruct((40, BLOCK), F32),
        ),
        in_specs=[hbm] * 5,
        out_specs=[vmem] * 2,
        scratch_shapes=[
            pltpu.VMEM((32, 64), F32),
            pltpu.VMEM((64, 64), F32),
            pltpu.VMEM((16, BLOCK), F32),
            pltpu.VMEM((16, BLOCK), jnp.int32),
            pltpu.VMEM((4, 16), jnp.int32),
            pltpu.VMEM((64, 16, BLOCK), F32),
            pltpu.VMEM((8, 32, BLOCK), F32),
            pltpu.VMEM((8, 256, 384), BF16),
            pltpu.VMEM((512, 384), BF16),
            pltpu.VMEM((8, 4, BLOCK, 256), F32),
            pltpu.VMEM((4, 16, BLOCK), F32),
            pltpu.VMEM((NA, 8, BLOCK), F32),
            pltpu.VMEM((NA, 8, BLOCK), F32),
            pltpu.VMEM((5, 16, BLOCK), F32),
            pltpu.VMEM((4, BLOCK, BLOCK), F32),
            pltpu.VMEM((2, 3, 16, BLOCK), F32),
            pltpu.VMEM((2, 3, 16, BLOCK), F32),
            pltpu.VMEM((2, 7, 16, BLOCK), F32),
            pltpu.VMEM((4, 16, BLOCK), F32),
            pltpu.SemaphoreType.DMA((N_SEM,)),
            pltpu.SemaphoreType.DMA((N_SEM,)),
            pltpu.SemaphoreType.DMA((5,)),
        ],
        compiler_params=pltpu.CompilerParams(
            collective_id=0, has_side_effects=True, vmem_limit_bytes=32 * 1024 * 1024
        ),
        name="exchange",
    )(
        *(
            pltpu.with_memory_space_constraint(operand, pltpu.HBM)
            for operand in (
                adv_embed,
                imp_embed,
                value_scale.reshape(16, BLOCK),
                spend_class.reshape(16, BLOCK),
                eligible.T,
            )
        )
    )
    density, prices, pacing = pl.pallas_call(
        scale_kernel,
        out_shape=(
            jax.ShapeDtypeStruct((2048, 512), F32),
            jax.ShapeDtypeStruct((4, BLOCK), F32),
            jax.ShapeDtypeStruct((16, BLOCK), F32),
        ),
        in_specs=[vmem] * 2,
        out_specs=[hbm] * 3,
        scratch_shapes=[
            pltpu.VMEM((2048, 512), F32),
            pltpu.SemaphoreType.DMA((10,)),
        ],
        compiler_params=pltpu.CompilerParams(vmem_limit_bytes=32 * 1024 * 1024),
        name="scale",
    )(gains, aux)
    return density, prices.reshape(512), pacing.reshape(2048)


def solution(mesh):
    in_specs = (
        P(("adv", "imp"), None),
        P(("imp", "adv"), None),
        P("adv"),
        P("adv"),
        P("adv", "imp"),
    )
    out_specs = (P("adv", "imp"), P("imp"), P("adv"))
    return jax.shard_map(
        per_device, mesh=mesh, in_specs=in_specs, out_specs=out_specs, check_vma=False
    )
```

```python
import functools

import jax
import jax.numpy as jnp
from jax import lax
from jax.experimental import pallas as pl
from jax.experimental.pallas import tpu as pltpu
from jax.sharding import PartitionSpec as P

MESH = pl.DeviceIdType.MESH
BLOCK = 128
SCORE_GAIN = 0.0875
LOG2E = 1.4426950408889634
NX = 4
NZ = 16
NA = 8
F32 = jnp.float32
BF16 = jnp.bfloat16

NEAR = (1, -1, 2, -2, 3, -3, 4, -4)
FAR_NEG = (1, 2, 3, 4)
FAR_POS = (1, 2, 3)
WINDOW = (1, -1, 2, -2)
JUMP = (5, -5)
ALL_D = (0, 1, -1, 2, -2, 3, -3, 4, -4, 5, -5, 6, -6, 7, -7, 8)

_n = 0
S_Z = {}
for _d in ALL_D[1:]:
    S_Z[_d] = _n
    _n += 1
S_X = {}
for _d in ALL_D:
    for _e in (1, 2, 3):
        S_X[_d, _e] = _n
        _n += 1
S_P1 = {}
S_P2 = {}
for _k in range(1, NA):
    S_P1[_k] = _n
    S_P2[_k] = _n + 1
    _n += 2
S_IX = {}
S_WX = {}
S_QX = {}
S_RX = {}
for _e in (1, 2, 3):
    S_IX[_e] = _n
    S_WX[_e] = _n + 1
    S_QX[_e] = _n + 2
    S_RX[_e] = _n + 3
    _n += 4
S_IY = {}
S_IC = {}
for _e in range(4):
    for _k in range(4):
        if _k:
            S_IY[_e, _k] = _n
            _n += 1
        S_IC[_e, _k] = _n
        _n += 1
S_QZ = {}
for _d in ALL_D[1:]:
    S_QZ[_d] = _n
    _n += 1
S_RZ = {}
for _d in WINDOW + JUMP + (8,):
    S_RZ[_d] = _n
    _n += 1
N_SEM = _n


def split_parts(rows):
    high = rows.astype(BF16).astype(F32)
    rest = rows - high
    mid = rest.astype(BF16).astype(F32)
    low = rest - mid
    return high, mid, low


def first_half(shape):
    return lax.broadcasted_iota(jnp.int32, shape, len(shape) - 1) < 64


def twice(packed):
    turned = pltpu.roll(packed, 64, axis=len(packed.shape) - 1)
    left = first_half(packed.shape)
    return jnp.where(left, packed, turned), jnp.where(left, turned, packed)


def exchange_kernel(
    adv_hbm,
    imp_hbm,
    scale_hbm,
    class_hbm,
    elig_hbm,
    g_ref,
    aux_ref,
    adv_in,
    imp_in,
    scale_ref,
    class_ref,
    elig_ref,
    adv_buf,
    imp_buf,
    a_ref,
    b_ref,
    e_ref,
    t_ref,
    p1_buf,
    p2_buf,
    wl_buf,
    quarter_buf,
    spend_buf,
    r1_ref,
    c2_ref,
    sums,
    rx_buf,
    rz_buf,
    w_ref,
    send_sem,
    recv_sem,
    in_sem,
):
    adv = lax.axis_index("adv")
    imp = lax.axis_index("imp")
    z = imp // NX
    x = lax.rem(imp, NX)

    def at_z(d):
        return lax.rem(z + (d + NZ), NZ)

    def at_x(e):
        return lax.rem(x + e, NX)

    def shard(d, e):
        return adv_buf.at[at_z(d), at_x(e)]

    partner = adv + 1 - 2 * lax.rem(adv, 2)

    def to_z(d):
        return (adv, at_z(d) * NX + x)

    def to_x(e):
        return (adv, z * NX + at_x(e))

    def to_adv(k):
        return (lax.rem(adv + k, NA), imp)

    def imps(e, whose, k):
        return imp_buf.at[at_x(NX - e), lax.rem(whose + (NA - 2 * k), NA)]

    started = []

    def remote(src, dst, number, device):
        return pltpu.make_async_remote_copy(
            src_ref=src,
            dst_ref=dst,
            send_sem=send_sem.at[number],
            recv_sem=recv_sem.at[number],
            device_id=device,
            device_id_type=MESH,
        )

    def send(src, dst, number, device):
        copy = remote(src, dst, number, device)
        copy.start()
        started.append(copy)

    def arrived(ref, number):
        remote(ref, ref, number, to_x(1)).wait_recv()

    loads = [
        pltpu.make_async_copy(src, dst, in_sem.at[n])
        for n, (src, dst) in enumerate(
            (
                (adv_hbm, adv_in),
                (imp_hbm, imp_in),
                (scale_hbm, scale_ref),
                (class_hbm, class_ref),
                (elig_hbm, elig_ref),
            )
        )
    ]
    for load in loads:
        load.start()

    barrier = pltpu.get_barrier_semaphore()
    peers = [to_z(d) for d in NEAR] + [to_x(e) for e in (1, 2, 3)] + [to_adv(k) for k in range(1, NA)]
    for device in peers:
        pl.semaphore_signal(barrier, inc=1, device_id=device, device_id_type=MESH)

    mine = shard(0, 0)
    loads[0].wait()
    adv_buf[z, x] = jnp.concatenate([adv_in[0:16, :], adv_in[16:32, :]], axis=1)
    loads[1].wait()
    imp_buf[x, adv] = jnp.concatenate([imp_in[0:32, :], imp_in[32:64, :]], axis=1)
    for load in loads[2:]:
        load.wait()
    allowance = 2.0 * jnp.exp(0.3 * class_ref[...].astype(F32) - 1.2)
    mask_rows = elig_ref[...].astype(F32)
    mask = mask_rows.T
    p1_buf[adv] = jnp.zeros((8, BLOCK), F32)
    for cb in range(4):
        p1_buf[adv, cb : cb + 1, :] = jnp.sum(allowance * mask[:, cb : cb + 1], axis=0, keepdims=True)

    pl.semaphore_wait(barrier, len(peers))

    for d in (4, -4, 3, -3, 2, -2, 1, -1):
        send(mine, mine, S_Z[-d], to_z(d))
    own = imps(0, adv, 0)
    for e in (2, 1, 3):
        send(own, own, S_IX[e], to_x(e))
    for k in (2, 1, 3):
        send(own, own, S_IY[0, k], to_adv(2 * k))
    send(own, own, S_IC[0, 0], (partner, imp))
    for k in range(1, NA):
        send(p1_buf.at[adv], p1_buf.at[adv], S_P1[k], to_adv(k))
    for e in (2, 1, 3):
        send(mine, mine, S_X[0, e], to_x(e))

    def pass_on(d):
        here = shard(d, 0)
        arrived(here, S_Z[d])
        if d == -4:
            for k in FAR_NEG:
                far = -4 - k
                send(here, here, S_Z[8 if far == -8 else far], to_z(k))
        if d == 4:
            for k in FAR_POS:
                send(here, here, S_Z[4 + k], to_z(-k))
        for e in (2, 1, 3):
            send(here, here, S_X[d, e], to_x(e))

    for d in (1, -1, 2, -2):
        pass_on(d)
    for e in (1, 3, 2):
        here = imps(e, adv, 0)
        arrived(here, S_IX[e])
        for k in (2, 1, 3):
            send(here, here, S_IY[e, k], to_adv(2 * k))
        send(here, here, S_IC[e, 0], (partner, imp))
    for d in (3, -3, 4, -4):
        pass_on(d)

    for k in range(1, NA):
        arrived(p1_buf.at[lax.rem(adv + (NA - k), NA)], S_P1[k])
    share = p1_buf[0]
    for k in range(1, NA):
        share = share + p1_buf[k]
    first_price = jnp.sum(share, axis=1, keepdims=True) / 32768.0
    weight_rows = mask_rows / first_price[0:4, :]
    place = lax.broadcasted_iota(jnp.int32, (4, BLOCK), 1) // 32
    for q in range(4):
        spread = jnp.zeros((4, BLOCK), F32)
        for k in range(4):
            spread = jnp.where(place == k, weight_rows[:, 4 * q + k : 4 * q + k + 1], spread)
        wl_buf[x, 4 * q : 4 * q + 4, :] = spread
    for e in (2, 1, 3):
        send(wl_buf.at[x], wl_buf.at[x], S_WX[e], to_x(e))
    for cb in range(4):
        w_ref[cb] = jnp.broadcast_to(mask[:, cb : cb + 1] / first_price[cb : cb + 1, :], (16, BLOCK))

    for e in (0, 1, 3, 2):
        for k in (1, 3, 2):
            here = imps(e, adv, k)
            arrived(here, S_IY[e, k])
            send(here, here, S_IC[e, k], (partner, imp))
    for e in range(4):
        for k in range(4):
            arrived(imps(e, partner, k), S_IC[e, k])

    @pl.loop(0, 4)
    def _(xp):
        low_half, up_half = twice(imp_buf[xp] * (SCORE_GAIN * LOG2E))
        doubled = jnp.concatenate([low_half, up_half], axis=1).reshape(512, BLOCK)
        high, mid, low = split_parts(doubled)
        left = first_half((512, BLOCK))
        b_ref[xp, :, 0:128] = jnp.where(left, high, mid).astype(BF16)
        b_ref[xp, :, 128:256] = jnp.where(left, high, low).astype(BF16)
        b_ref[xp, :, 256:384] = jnp.where(left, mid, high).astype(BF16)

    def operand(shards):
        low_half, up_half = twice(shards)
        doubled = jnp.concatenate([low_half, up_half], axis=1).reshape(shards.shape[0] * 32, BLOCK)
        high, mid, low = split_parts(doubled)
        left = first_half(doubled.shape)
        return jnp.concatenate(
            [
                high.astype(BF16),
                jnp.where(left, mid, high).astype(BF16),
                jnp.where(left, mid, low).astype(BF16),
            ],
            axis=1,
        )

    def exp_scores(left_rows, right_rows):
        scores = lax.dot_general(
            left_rows, right_rows, (((1,), (1,)), ((), ())), preferred_element_type=F32
        )
        return jnp.exp2(scores)

    def quad(q):
        rows = operand(adv_buf[pl.ds(q * 4, 4), x])
        total = jnp.zeros((8, BLOCK), F32)
        for xp in range(4):
            values = exp_scores(b_ref[xp], rows).reshape(4, 16, 8, BLOCK)
            for cb in range(4):
                total = total + jnp.sum(values[cb], axis=0) * wl_buf[xp, pl.ds(q * 4 + cb, 1), :]
        quarter_buf[z, pl.ds(q, 1), :] = jnp.sum(total, axis=0, keepdims=True)

    for e in (1, 3, 2):
        arrived(wl_buf.at[at_x(NX - e)], S_WX[e])
    my_quad = z // 4

    @pl.loop(0, 1)
    def _(n):
        quad(my_quad + n)

    for d in (5, -5, 6, -6, 7, -7, 8):
        pass_on(d)

    @pl.loop(1, 4)
    def _(n):
        quad(lax.rem(my_quad + n, 4))

    for d in reversed(ALL_D[1:]):
        send(quarter_buf.at[z], quarter_buf.at[z], S_QZ[d], to_z(-d))

    for d in ALL_D:
        for e in (1, 2, 3):
            arrived(shard(d, NX - e), S_X[d, e])

    @pl.loop(0, 8)
    def _(p):
        rows = operand(adv_buf[pl.ds(p * 2, 2)].reshape(8, 16, BLOCK))
        a_ref[p] = rows
        for cb in range(4):
            e_ref[p, cb] = exp_scores(b_ref[x, cb * BLOCK : cb * BLOCK + BLOCK, :], rows)

    def tile_values(start, stop):
        @pl.loop(start, stop)
        def _(p):
            g_ref[pl.ds(pl.multiple_of(p * 256, 256), 256), :] = exp_scores(a_ref[p], b_ref[x])

    tile_values(0, 3)
    for d in ALL_D[1:]:
        arrived(quarter_buf.at[at_z(d)], S_QZ[d])
    spent = quarter_buf[0]
    for other in range(1, NZ):
        spent = spent + quarter_buf[other]

    for k in range(4):
        turned = pltpu.roll(spent, lax.rem(x - k + 4, 4) * 32, axis=1)
        turned = jnp.where(place == x, turned, 0.0)
        for q in range(4):
            spend_buf[x, 4 * q + k : 4 * q + k + 1, :] = turned[q : q + 1, :]
    for e in (2, 1, 3):
        send(spend_buf.at[x], spend_buf.at[x], S_QX[e], to_x(e))
    tile_values(3, 8)
    for e in (1, 3, 2):
        arrived(spend_buf.at[at_x(NX - e)], S_QX[e])

    scale = scale_ref[...]
    first_bid = allowance * scale / 32768.0
    spending = ((spend_buf[0] + spend_buf[1]) + (spend_buf[2] + spend_buf[3])) * first_bid
    pacing = allowance / jnp.maximum(spending, allowance)
    row_bid = first_bid * pacing
    for cb in range(4):
        r1_ref[cb] = row_bid * w_ref[cb]
    r1_ref[4] = row_bid

    mine_p2 = p2_buf.at[adv]
    p2_buf[adv] = jnp.ones((8, BLOCK), F32)
    for cb in range(4):
        total = None
        for rb in range(16):
            row = r1_ref[cb, rb : rb + 1, :]
            half = rb % 2
            term = e_ref[rb // 2, cb, :, half * 128 : half * 128 + 128] * row
            total = term if total is None else total + term
        p2_buf[adv, cb : cb + 1, :] = jnp.sum(total.T, axis=0, keepdims=True)

    for k in range(1, NA):
        send(mine_p2, mine_p2, S_P2[k], to_adv(k))

    @pl.loop(0, 8)
    def _(p):
        for half in range(2):
            for cb in range(4):
                row = r1_ref[cb, pl.ds(2 * p + half, 1), :]
                value = e_ref[p, cb, :, half * 128 : half * 128 + 128]
                e_ref[p, cb, :, half * 128 : half * 128 + 128] = (value * row) * value

    for k in range(1, NA):
        arrived(p2_buf.at[lax.rem(adv + (NA - k), NA)], S_P2[k])
    price = p2_buf[0]
    for k in range(1, NA):
        price = price + p2_buf[k]
    inverse = 1.0 / price
    for cb in range(4):
        c2_ref[cb] = jnp.broadcast_to(inverse[cb : cb + 1, :], (BLOCK, BLOCK)).T

    @pl.loop(0, 8)
    def _(p):
        for half in range(2):
            total = jnp.zeros((8, BLOCK), F32)
            for cb in range(4):
                gain = e_ref[p, cb, :, half * 128 : half * 128 + 128] * c2_ref[cb]
                total = total + jnp.sum(gain.reshape(16, 8, BLOCK), axis=0)
            t_ref[pl.ds(2 * p + half, 1), :] = jnp.sum(total, axis=0, keepdims=True)

    def tile_gains(start, stop):
        @pl.loop(start, stop)
        def _(p):
            for half in range(2):
                rb = 2 * p + half
                rows = pl.ds(pl.multiple_of(p * 256 + half * 128, 128), 128)
                first = jnp.broadcast_to(r1_ref[4, pl.ds(rb, 1), :], (BLOCK, BLOCK)).T
                for cb in range(4):
                    value = g_ref[rows, cb * 128 : cb * 128 + 128]
                    bid = value * (first * w_ref[cb, pl.ds(rb, 1), :])
                    g_ref[rows, cb * 128 : cb * 128 + 128] = bid * inverse[cb : cb + 1, :] * value

    part = t_ref[...]
    sums[0] = part
    for e in (2, 1, 3):
        send(sums.at[0], rx_buf.at[e - 1], S_RX[e], to_x(e))
    tile_gains(0, 2)
    for e in (1, 3, 2):
        arrived(rx_buf.at[e - 1], S_RX[e])
    total = part + rx_buf[1] + (rx_buf[0] + rx_buf[2])
    sums[1] = total
    index = {d: i for i, d in enumerate(WINDOW + JUMP + (8,))}
    for d in (2, -2, 1, -1, 8):
        send(sums.at[1], rz_buf.at[index[d]], S_RZ[d], to_z(-d))
    tile_gains(2, 4)
    for d in WINDOW:
        arrived(rz_buf.at[index[d]], S_RZ[d])
    window = total + ((rz_buf[0] + rz_buf[1]) + (rz_buf[2] + rz_buf[3]))
    sums[2] = window
    for d in JUMP:
        send(sums.at[2], rz_buf.at[index[d]], S_RZ[d], to_z(-d))
    tile_gains(4, 8)
    for copy in started:
        copy.wait_send()
    for d in JUMP + (8,):
        arrived(rz_buf.at[index[d]], S_RZ[d])
    spending = (window + (rz_buf[4] + rz_buf[5]) + rz_buf[6]) * scale
    pacing = allowance / jnp.maximum(spending, allowance)
    aux_ref[0:16] = scale * pacing * 16384.0
    aux_ref[16:32] = pacing
    aux_ref[32:40] = price


def scale_kernel(g_ref, aux_ref, out_hbm, price_hbm, pacing_hbm, out_ref, sem):
    small = [
        pltpu.make_async_copy(aux_ref.at[32:36], price_hbm, sem.at[8]),
        pltpu.make_async_copy(aux_ref.at[16:32], pacing_hbm, sem.at[9]),
    ]
    copies = []
    for p in range(8):
        for half in range(2):
            rb = 2 * p + half
            column = jnp.broadcast_to(aux_ref[rb : rb + 1, :], (BLOCK, BLOCK)).T
            rows = slice(rb * 128, rb * 128 + 128)
            for cb in range(4):
                columns = slice(cb * 128, cb * 128 + 128)
                out_ref[rows, columns] = g_ref[rows, columns] * column
        span = slice(p * 256, p * 256 + 256)
        copies.append(pltpu.make_async_copy(out_ref.at[span], out_hbm.at[span], sem.at[p]))
        copies[-1].start()
    for copy in small:
        copy.start()
    for copy in copies + small:
        copy.wait()


def per_device(adv_embed, imp_embed, value_scale, spend_class, eligible):
    hbm = pl.BlockSpec(memory_space=pltpu.HBM)
    vmem = pl.BlockSpec(memory_space=pltpu.VMEM)
    gains, aux = pl.pallas_call(
        exchange_kernel,
        out_shape=(
            jax.ShapeDtypeStruct((2048, 512), F32),
            jax.ShapeDtypeStruct((40, BLOCK), F32),
        ),
        in_specs=[hbm] * 5,
        out_specs=[vmem] * 2,
        scratch_shapes=[
            pltpu.VMEM((32, 64), F32),
            pltpu.VMEM((64, 64), F32),
            pltpu.VMEM((16, BLOCK), F32),
            pltpu.VMEM((16, BLOCK), jnp.int32),
            pltpu.VMEM((4, 16), jnp.int32),
            pltpu.VMEM((NZ, NX, 16, BLOCK), F32),
            pltpu.VMEM((NX, NA, 32, BLOCK), F32),
            pltpu.VMEM((8, 256, 384), BF16),
            pltpu.VMEM((NX, 512, 384), BF16),
            pltpu.VMEM((8, 4, BLOCK, 256), F32),
            pltpu.VMEM((16, BLOCK), F32),
            pltpu.VMEM((NA, 8, BLOCK), F32),
            pltpu.VMEM((NA, 8, BLOCK), F32),
            pltpu.VMEM((NX, 16, BLOCK), F32),
            pltpu.VMEM((NZ, 4, BLOCK), F32),
            pltpu.VMEM((NX, 16, BLOCK), F32),
            pltpu.VMEM((5, 16, BLOCK), F32),
            pltpu.VMEM((4, BLOCK, BLOCK), F32),
            pltpu.VMEM((3, 16, BLOCK), F32),
            pltpu.VMEM((3, 16, BLOCK), F32),
            pltpu.VMEM((7, 16, BLOCK), F32),
            pltpu.VMEM((4, 16, BLOCK), F32),
            pltpu.SemaphoreType.DMA((N_SEM,)),
            pltpu.SemaphoreType.DMA((N_SEM,)),
            pltpu.SemaphoreType.DMA((5,)),
        ],
        compiler_params=pltpu.CompilerParams(
            collective_id=0, has_side_effects=True, vmem_limit_bytes=32 * 1024 * 1024
        ),
        name="exchange",
    )(
        *(
            pltpu.with_memory_space_constraint(operand, pltpu.HBM)
            for operand in (
                adv_embed,
                imp_embed,
                value_scale.reshape(16, BLOCK),
                spend_class.reshape(16, BLOCK),
                eligible.T,
            )
        )
    )
    density, prices, pacing = pl.pallas_call(
        scale_kernel,
        out_shape=(
            jax.ShapeDtypeStruct((2048, 512), F32),
            jax.ShapeDtypeStruct((4, BLOCK), F32),
            jax.ShapeDtypeStruct((16, BLOCK), F32),
        ),
        in_specs=[vmem] * 2,
        out_specs=[hbm] * 3,
        scratch_shapes=[
            pltpu.VMEM((2048, 512), F32),
            pltpu.SemaphoreType.DMA((10,)),
        ],
        compiler_params=pltpu.CompilerParams(vmem_limit_bytes=32 * 1024 * 1024),
        name="scale",
    )(gains, aux)
    return density, prices.reshape(512), pacing.reshape(2048)


def solution(mesh):
    in_specs = (
        P(("adv", "imp"), None),
        P(("imp", "adv"), None),
        P("adv"),
        P("adv"),
        P("adv", "imp"),
    )
    out_specs = (P("adv", "imp"), P("imp"), P("adv"))
    return jax.shard_map(
        per_device, mesh=mesh, in_specs=in_specs, out_specs=out_specs, check_vma=False
    )
```

```python
import functools

import jax
import jax.numpy as jnp
from jax import lax
from jax.experimental import pallas as pl
from jax.experimental.pallas import tpu as pltpu
from jax.sharding import PartitionSpec as P

MESH = pl.DeviceIdType.MESH
BLOCK = 128
SCORE_GAIN = 0.0875
LOG2E = 1.4426950408889634
NX = 4
NZ = 16
NA = 8
F32 = jnp.float32
BF16 = jnp.bfloat16

FAR_Z = (5, -5, 6, -6, 7, -7, 8)
NEAR = (1, -1, 2, -2, 3, -3, 4, -4)
FAR_NEG = (1, 2, 3, 4)
FAR_POS = (1, 2, 3)
WINDOW = (1, -1, 2, -2)
JUMP = (5, -5)
ALL_D = (0, 1, -1, 2, -2, 3, -3, 4, -4, 5, -5, 6, -6, 7, -7, 8)

_n = 0
S_Z = {}
for _d in ALL_D[1:]:
    S_Z[_d] = _n
    _n += 1
S_X = {}
for _d in ALL_D:
    for _e in (1, 2, 3):
        S_X[_d, _e] = _n
        _n += 1
S_P1 = {}
S_P2 = {}
for _k in range(1, NA):
    S_P1[_k] = _n
    S_P2[_k] = _n + 1
    _n += 2
S_IX = {}
S_WX = {}
S_QX = {}
S_RX = {}
for _e in (1, 2, 3):
    S_IX[_e] = _n
    S_WX[_e] = _n + 1
    S_QX[_e] = _n + 2
    S_RX[_e] = _n + 3
    _n += 4
S_IY = {}
S_IC = {}
for _e in range(4):
    for _k in range(4):
        if _k:
            S_IY[_e, _k] = _n
            _n += 1
        S_IC[_e, _k] = _n
        _n += 1
S_QZ = {}
for _d in ALL_D[1:]:
    S_QZ[_d] = _n
    _n += 1
S_RZ = {}
for _d in WINDOW + JUMP + (8,):
    S_RZ[_d] = _n
    _n += 1
N_SEM = _n


def split_parts(rows):
    high = rows.astype(BF16).astype(F32)
    rest = rows - high
    mid = rest.astype(BF16).astype(F32)
    low = rest - mid
    return high, mid, low


def first_half(shape):
    return lax.broadcasted_iota(jnp.int32, shape, len(shape) - 1) < 64


def twice(packed):
    turned = pltpu.roll(packed, 64, axis=len(packed.shape) - 1)
    left = first_half(packed.shape)
    return jnp.where(left, packed, turned), jnp.where(left, turned, packed)


def exchange_kernel(
    adv_hbm,
    imp_hbm,
    scale_hbm,
    class_hbm,
    elig_hbm,
    g_ref,
    aux_ref,
    adv_in,
    imp_in,
    scale_ref,
    class_ref,
    elig_ref,
    adv_buf,
    imp_buf,
    a_ref,
    column_ref,
    b_ref,
    e_ref,
    t_ref,
    p1_buf,
    p2_buf,
    wl_buf,
    quarter_buf,
    spend_buf,
    r1_ref,
    c2_ref,
    sums,
    rx_buf,
    rz_buf,
    w_ref,
    send_sem,
    recv_sem,
    in_sem,
):
    adv = lax.axis_index("adv")
    imp = lax.axis_index("imp")
    z = imp // NX
    x = lax.rem(imp, NX)

    def at_z(d):
        return lax.rem(z + (d + NZ), NZ)

    def at_x(e):
        return lax.rem(x + e, NX)

    def shard(d, e):
        return adv_buf.at[at_z(d), at_x(e)]

    partner = adv + 1 - 2 * lax.rem(adv, 2)

    def to_z(d):
        return (adv, at_z(d) * NX + x)

    def to_x(e):
        return (adv, z * NX + at_x(e))

    def to_adv(k):
        return (lax.rem(adv + k, NA), imp)

    def imps(e, whose, k):
        return imp_buf.at[at_x(NX - e), lax.rem(whose + (NA - 2 * k), NA)]

    started = []

    def remote(src, dst, number, device):
        return pltpu.make_async_remote_copy(
            src_ref=src,
            dst_ref=dst,
            send_sem=send_sem.at[number],
            recv_sem=recv_sem.at[number],
            device_id=device,
            device_id_type=MESH,
        )

    def send(src, dst, number, device):
        copy = remote(src, dst, number, device)
        copy.start()
        started.append(copy)

    def arrived(ref, number):
        remote(ref, ref, number, to_x(1)).wait_recv()

    loads = [
        pltpu.make_async_copy(src, dst, in_sem.at[n])
        for n, (src, dst) in enumerate(
            (
                (adv_hbm, adv_in),
                (imp_hbm, imp_in),
                (scale_hbm, scale_ref),
                (class_hbm, class_ref),
                (elig_hbm, elig_ref),
            )
        )
    ]
    for load in loads:
        load.start()

    barrier = pltpu.get_barrier_semaphore()
    peers = [to_z(d) for d in NEAR] + [to_x(e) for e in (1, 2, 3)] + [to_adv(k) for k in range(1, NA)]
    for device in peers:
        pl.semaphore_signal(barrier, inc=1, device_id=device, device_id_type=MESH)

    mine = shard(0, 0)
    loads[0].wait()
    adv_buf[z, x] = jnp.concatenate([adv_in[0:16, :], adv_in[16:32, :]], axis=1)
    loads[1].wait()
    imp_buf[x, adv] = jnp.concatenate([imp_in[0:32, :], imp_in[32:64, :]], axis=1)
    for load in loads[2:]:
        load.wait()
    allowance = 2.0 * jnp.exp(0.3 * class_ref[...].astype(F32) - 1.2)
    mask_rows = elig_ref[...].astype(F32)
    mask = mask_rows.T
    p1_buf[adv] = jnp.zeros((8, BLOCK), F32)
    for cb in range(4):
        p1_buf[adv, cb : cb + 1, :] = jnp.sum(allowance * mask[:, cb : cb + 1], axis=0, keepdims=True)

    pl.semaphore_wait(barrier, len(peers))

    for d in (4, -4, 3, -3, 2, -2, 1, -1):
        send(mine, mine, S_Z[-d], to_z(d))
    own = imps(0, adv, 0)
    for e in (2, 1, 3):
        send(own, own, S_IX[e], to_x(e))
    for k in (2, 1, 3):
        send(own, own, S_IY[0, k], to_adv(2 * k))
    send(own, own, S_IC[0, 0], (partner, imp))
    for k in range(1, NA):
        send(p1_buf.at[adv], p1_buf.at[adv], S_P1[k], to_adv(k))
    for e in (2, 1, 3):
        send(mine, mine, S_X[0, e], to_x(e))

    def pass_on(d):
        here = shard(d, 0)
        arrived(here, S_Z[d])
        if d == -4:
            for k in FAR_NEG:
                far = -4 - k
                send(here, here, S_Z[8 if far == -8 else far], to_z(k))
        if d == 4:
            for k in FAR_POS:
                send(here, here, S_Z[4 + k], to_z(-k))
        for e in (2, 1, 3):
            send(here, here, S_X[d, e], to_x(e))

    for d in (1, -1, 2, -2):
        pass_on(d)
    for e in (1, 3, 2):
        here = imps(e, adv, 0)
        arrived(here, S_IX[e])
        for k in (2, 1, 3):
            send(here, here, S_IY[e, k], to_adv(2 * k))
        send(here, here, S_IC[e, 0], (partner, imp))
    for d in (3, -3, 4, -4):
        pass_on(d)

    for k in range(1, NA):
        arrived(p1_buf.at[lax.rem(adv + (NA - k), NA)], S_P1[k])
    share = p1_buf[0]
    for k in range(1, NA):
        share = share + p1_buf[k]
    first_price = jnp.sum(share, axis=1, keepdims=True) / 32768.0
    weight_rows = mask_rows / first_price[0:4, :]
    place = lax.broadcasted_iota(jnp.int32, (4, BLOCK), 1) // 32
    for q in range(4):
        spread = jnp.zeros((4, BLOCK), F32)
        for k in range(4):
            spread = jnp.where(place == k, weight_rows[:, 4 * q + k : 4 * q + k + 1], spread)
        wl_buf[x, 4 * q : 4 * q + 4, :] = spread
    for e in (2, 1, 3):
        send(wl_buf.at[x], wl_buf.at[x], S_WX[e], to_x(e))
    for cb in range(4):
        w_ref[cb] = jnp.broadcast_to(mask[:, cb : cb + 1] / first_price[cb : cb + 1, :], (16, BLOCK))

    for e in (0, 1, 3, 2):
        for k in (1, 3, 2):
            here = imps(e, adv, k)
            arrived(here, S_IY[e, k])
            send(here, here, S_IC[e, k], (partner, imp))
    def prepare(xp):
        low_half, up_half = twice(imp_buf[xp] * (SCORE_GAIN * LOG2E))
        doubled = jnp.concatenate([low_half, up_half], axis=1).reshape(512, BLOCK)
        high, mid, low = split_parts(doubled)
        left = first_half((512, BLOCK))
        b_ref[xp, :, 0:128] = jnp.where(left, high, mid).astype(BF16)
        b_ref[xp, :, 128:256] = jnp.where(left, high, low).astype(BF16)
        b_ref[xp, :, 256:384] = jnp.where(left, mid, high).astype(BF16)

    def operand(shards):
        low_half, up_half = twice(shards)
        doubled = jnp.concatenate([low_half, up_half], axis=1).reshape(shards.shape[0] * 32, BLOCK)
        high, mid, low = split_parts(doubled)
        left = first_half(doubled.shape)
        return jnp.concatenate(
            [
                high.astype(BF16),
                jnp.where(left, mid, high).astype(BF16),
                jnp.where(left, mid, low).astype(BF16),
            ],
            axis=1,
        )

    def exp_scores(left_rows, right_rows):
        scores = lax.dot_general(
            left_rows, right_rows, (((1,), (1,)), ((), ())), preferred_element_type=F32
        )
        return jnp.exp2(scores)

    for e in (1, 3, 2):
        arrived(wl_buf.at[at_x(NX - e)], S_WX[e])
    for e in (0, 1, 3, 2):
        for k in range(4):
            arrived(imps(e, partner, k), S_IC[e, k])
        prepare(at_x(NX - e))
    for d in FAR_Z:
        pass_on(d)
    column_ref[...] = operand(adv_buf[:, x])
    totals = [jnp.zeros((8, BLOCK), F32) for _ in range(4)]
    for e in (0, 1, 3, 2):
        xp = at_x(NX - e)
        for cb in range(4):
            values = exp_scores(b_ref[xp, cb * BLOCK : cb * BLOCK + BLOCK, :], column_ref[...])
            values = jnp.sum(values.reshape(16, 8, 512), axis=0)
            for q in range(4):
                row = wl_buf[xp, 4 * q + cb : 4 * q + cb + 1, :]
                totals[q] = totals[q] + values[:, q * 128 : q * 128 + 128] * row
    for q in range(4):
        quarter_buf[z, q : q + 1, :] = jnp.sum(totals[q], axis=0, keepdims=True)

    for d in reversed(ALL_D[1:]):
        send(quarter_buf.at[z], quarter_buf.at[z], S_QZ[d], to_z(-d))

    for d in ALL_D:
        for e in (1, 2, 3):
            arrived(shard(d, NX - e), S_X[d, e])

    @pl.loop(0, 8)
    def _(p):
        rows = operand(adv_buf[pl.ds(p * 2, 2)].reshape(8, 16, BLOCK))
        a_ref[p] = rows
        for cb in range(4):
            e_ref[p, cb] = exp_scores(b_ref[x, cb * BLOCK : cb * BLOCK + BLOCK, :], rows)

    def tile_values(start, stop):
        @pl.loop(start, stop)
        def _(p):
            g_ref[pl.ds(pl.multiple_of(p * 256, 256), 256), :] = exp_scores(a_ref[p], b_ref[x])

    for d in ALL_D[1:]:
        arrived(quarter_buf.at[at_z(d)], S_QZ[d])
    spent = quarter_buf[0]
    for other in range(1, NZ):
        spent = spent + quarter_buf[other]

    for k in range(4):
        turned = pltpu.roll(spent, lax.rem(x - k + 4, 4) * 32, axis=1)
        turned = jnp.where(place == x, turned, 0.0)
        for q in range(4):
            spend_buf[x, 4 * q + k : 4 * q + k + 1, :] = turned[q : q + 1, :]
    for e in (2, 1, 3):
        send(spend_buf.at[x], spend_buf.at[x], S_QX[e], to_x(e))
    for e in (1, 3, 2):
        arrived(spend_buf.at[at_x(NX - e)], S_QX[e])

    scale = scale_ref[...]
    first_bid = allowance * scale / 32768.0
    spending = ((spend_buf[0] + spend_buf[1]) + (spend_buf[2] + spend_buf[3])) * first_bid
    pacing = allowance / jnp.maximum(spending, allowance)
    row_bid = first_bid * pacing
    for cb in range(4):
        r1_ref[cb] = row_bid * w_ref[cb]
    r1_ref[4] = row_bid

    mine_p2 = p2_buf.at[adv]
    p2_buf[adv] = jnp.ones((8, BLOCK), F32)
    for cb in range(4):
        total = None
        for rb in range(16):
            row = r1_ref[cb, rb : rb + 1, :]
            half = rb % 2
            term = e_ref[rb // 2, cb, :, half * 128 : half * 128 + 128] * row
            total = term if total is None else total + term
        p2_buf[adv, cb : cb + 1, :] = jnp.sum(total.T, axis=0, keepdims=True)

    for k in range(1, NA):
        send(mine_p2, mine_p2, S_P2[k], to_adv(k))

    @pl.loop(0, 8)
    def _(p):
        for half in range(2):
            for cb in range(4):
                row = r1_ref[cb, pl.ds(2 * p + half, 1), :]
                value = e_ref[p, cb, :, half * 128 : half * 128 + 128]
                e_ref[p, cb, :, half * 128 : half * 128 + 128] = (value * row) * value

    for k in range(1, NA):
        arrived(p2_buf.at[lax.rem(adv + (NA - k), NA)], S_P2[k])
    price = p2_buf[0]
    for k in range(1, NA):
        price = price + p2_buf[k]
    inverse = 1.0 / price
    for cb in range(4):
        c2_ref[cb] = jnp.broadcast_to(inverse[cb : cb + 1, :], (BLOCK, BLOCK)).T

    @pl.loop(0, 8)
    def _(p):
        for half in range(2):
            total = jnp.zeros((8, BLOCK), F32)
            for cb in range(4):
                gain = e_ref[p, cb, :, half * 128 : half * 128 + 128] * c2_ref[cb]
                total = total + jnp.sum(gain.reshape(16, 8, BLOCK), axis=0)
            t_ref[pl.ds(2 * p + half, 1), :] = jnp.sum(total, axis=0, keepdims=True)

    def tile_gains(start, stop):
        @pl.loop(start, stop)
        def _(p):
            for half in range(2):
                rb = 2 * p + half
                rows = pl.ds(pl.multiple_of(p * 256 + half * 128, 128), 128)
                first = jnp.broadcast_to(r1_ref[4, pl.ds(rb, 1), :], (BLOCK, BLOCK)).T
                for cb in range(4):
                    value = g_ref[rows, cb * 128 : cb * 128 + 128]
                    bid = value * (first * w_ref[cb, pl.ds(rb, 1), :])
                    g_ref[rows, cb * 128 : cb * 128 + 128] = bid * inverse[cb : cb + 1, :] * value

    part = t_ref[...]
    sums[0] = part
    for e in (2, 1, 3):
        send(sums.at[0], rx_buf.at[e - 1], S_RX[e], to_x(e))
    tile_values(0, 8)
    for e in (1, 3, 2):
        arrived(rx_buf.at[e - 1], S_RX[e])
    total = part + rx_buf[1] + (rx_buf[0] + rx_buf[2])
    sums[1] = total
    index = {d: i for i, d in enumerate(WINDOW + JUMP + (8,))}
    for d in (2, -2, 1, -1, 8):
        send(sums.at[1], rz_buf.at[index[d]], S_RZ[d], to_z(-d))
    tile_gains(0, 4)
    for d in WINDOW:
        arrived(rz_buf.at[index[d]], S_RZ[d])
    window = total + ((rz_buf[0] + rz_buf[1]) + (rz_buf[2] + rz_buf[3]))
    sums[2] = window
    for d in JUMP:
        send(sums.at[2], rz_buf.at[index[d]], S_RZ[d], to_z(-d))
    tile_gains(4, 8)
    for copy in started:
        copy.wait_send()
    for d in JUMP + (8,):
        arrived(rz_buf.at[index[d]], S_RZ[d])
    spending = (window + (rz_buf[4] + rz_buf[5]) + rz_buf[6]) * scale
    pacing = allowance / jnp.maximum(spending, allowance)
    aux_ref[0:16] = scale * pacing * 16384.0
    aux_ref[16:32] = pacing
    aux_ref[32:40] = price


def scale_kernel(g_ref, aux_ref, out_hbm, price_hbm, pacing_hbm, out_ref, sem):
    small = [
        pltpu.make_async_copy(aux_ref.at[32:36], price_hbm, sem.at[8]),
        pltpu.make_async_copy(aux_ref.at[16:32], pacing_hbm, sem.at[9]),
    ]
    copies = []
    for p in range(8):
        for half in range(2):
            rb = 2 * p + half
            column = jnp.broadcast_to(aux_ref[rb : rb + 1, :], (BLOCK, BLOCK)).T
            rows = slice(rb * 128, rb * 128 + 128)
            for cb in range(4):
                columns = slice(cb * 128, cb * 128 + 128)
                out_ref[rows, columns] = g_ref[rows, columns] * column
        span = slice(p * 256, p * 256 + 256)
        copies.append(pltpu.make_async_copy(out_ref.at[span], out_hbm.at[span], sem.at[p]))
        copies[-1].start()
    for copy in small:
        copy.start()
    for copy in copies + small:
        copy.wait()


def per_device(adv_embed, imp_embed, value_scale, spend_class, eligible):
    hbm = pl.BlockSpec(memory_space=pltpu.HBM)
    vmem = pl.BlockSpec(memory_space=pltpu.VMEM)
    gains, aux = pl.pallas_call(
        exchange_kernel,
        out_shape=(
            jax.ShapeDtypeStruct((2048, 512), F32),
            jax.ShapeDtypeStruct((40, BLOCK), F32),
        ),
        in_specs=[hbm] * 5,
        out_specs=[vmem] * 2,
        scratch_shapes=[
            pltpu.VMEM((32, 64), F32),
            pltpu.VMEM((64, 64), F32),
            pltpu.VMEM((16, BLOCK), F32),
            pltpu.VMEM((16, BLOCK), jnp.int32),
            pltpu.VMEM((4, 16), jnp.int32),
            pltpu.VMEM((NZ, NX, 16, BLOCK), F32),
            pltpu.VMEM((NX, NA, 32, BLOCK), F32),
            pltpu.VMEM((8, 256, 384), BF16),
            pltpu.VMEM((512, 384), BF16),
            pltpu.VMEM((NX, 512, 384), BF16),
            pltpu.VMEM((8, 4, BLOCK, 256), F32),
            pltpu.VMEM((16, BLOCK), F32),
            pltpu.VMEM((NA, 8, BLOCK), F32),
            pltpu.VMEM((NA, 8, BLOCK), F32),
            pltpu.VMEM((NX, 16, BLOCK), F32),
            pltpu.VMEM((NZ, 4, BLOCK), F32),
            pltpu.VMEM((NX, 16, BLOCK), F32),
            pltpu.VMEM((5, 16, BLOCK), F32),
            pltpu.VMEM((4, BLOCK, BLOCK), F32),
            pltpu.VMEM((3, 16, BLOCK), F32),
            pltpu.VMEM((3, 16, BLOCK), F32),
            pltpu.VMEM((7, 16, BLOCK), F32),
            pltpu.VMEM((4, 16, BLOCK), F32),
            pltpu.SemaphoreType.DMA((N_SEM,)),
            pltpu.SemaphoreType.DMA((N_SEM,)),
            pltpu.SemaphoreType.DMA((5,)),
        ],
        compiler_params=pltpu.CompilerParams(
            collective_id=0, has_side_effects=True, vmem_limit_bytes=32 * 1024 * 1024
        ),
        name="exchange",
    )(
        *(
            pltpu.with_memory_space_constraint(operand, pltpu.HBM)
            for operand in (
                adv_embed,
                imp_embed,
                value_scale.reshape(16, BLOCK),
                spend_class.reshape(16, BLOCK),
                eligible.T,
            )
        )
    )
    density, prices, pacing = pl.pallas_call(
        scale_kernel,
        out_shape=(
            jax.ShapeDtypeStruct((2048, 512), F32),
            jax.ShapeDtypeStruct((4, BLOCK), F32),
            jax.ShapeDtypeStruct((16, BLOCK), F32),
        ),
        in_specs=[vmem] * 2,
        out_specs=[hbm] * 3,
        scratch_shapes=[
            pltpu.VMEM((2048, 512), F32),
            pltpu.SemaphoreType.DMA((10,)),
        ],
        compiler_params=pltpu.CompilerParams(vmem_limit_bytes=32 * 1024 * 1024),
        name="scale",
    )(gains, aux)
    return density, prices.reshape(512), pacing.reshape(2048)


def solution(mesh):
    in_specs = (
        P(("adv", "imp"), None),
        P(("imp", "adv"), None),
        P("adv"),
        P("adv"),
        P("adv", "imp"),
    )
    out_specs = (P("adv", "imp"), P("imp"), P("adv"))
    return jax.shard_map(
        per_device, mesh=mesh, in_specs=in_specs, out_specs=out_specs, check_vma=False
    )
```

```python
import functools

import jax
import jax.numpy as jnp
from jax import lax
from jax.experimental import pallas as pl
from jax.experimental.pallas import tpu as pltpu
from jax.sharding import PartitionSpec as P

MESH = pl.DeviceIdType.MESH
BLOCK = 128
SCORE_GAIN = 0.0875
LOG2E = 1.4426950408889634
NX = 4
NZ = 16
NA = 8
F32 = jnp.float32
BF16 = jnp.bfloat16

FAR_Z = (5, -5, 6, -6, 7, -7, 8)
NEAR = (1, -1, 2, -2, 3, -3, 4, -4)
FAR_NEG = (1, 2, 3, 4)
FAR_POS = (1, 2, 3)
WINDOW = (1, -1, 2, -2)
JUMP = (5, -5)
ALL_D = (0, 1, -1, 2, -2, 3, -3, 4, -4, 5, -5, 6, -6, 7, -7, 8)

_n = 0
S_Z = {}
for _d in ALL_D[1:]:
    S_Z[_d] = _n
    _n += 1
S_X = {}
for _d in ALL_D:
    for _e in (1, 2, 3):
        S_X[_d, _e] = _n
        _n += 1
S_P1 = {}
S_P2 = {}
for _k in range(1, NA):
    S_P1[_k] = _n
    S_P2[_k] = _n + 1
    _n += 2
S_IX = {}
S_WX = {}
S_QX = {}
S_RX = {}
for _e in (1, 2, 3):
    S_IX[_e] = _n
    S_WX[_e] = _n + 1
    S_QX[_e] = _n + 2
    S_RX[_e] = _n + 3
    _n += 4
S_IY = {}
S_IC = {}
for _e in range(4):
    for _k in range(4):
        if _k:
            S_IY[_e, _k] = _n
            _n += 1
        S_IC[_e, _k] = _n
        _n += 1
S_QZ = {}
for _d in ALL_D[1:]:
    S_QZ[_d] = _n
    _n += 1
S_RZ = {}
for _d in WINDOW + JUMP + (8,):
    S_RZ[_d] = _n
    _n += 1
N_SEM = _n


def split_parts(rows):
    high = rows.astype(BF16).astype(F32)
    rest = rows - high
    mid = rest.astype(BF16).astype(F32)
    low = rest - mid
    return high, mid, low


def first_half(shape):
    return lax.broadcasted_iota(jnp.int32, shape, len(shape) - 1) < 64


def twice(packed):
    turned = pltpu.roll(packed, 64, axis=len(packed.shape) - 1)
    left = first_half(packed.shape)
    return jnp.where(left, packed, turned), jnp.where(left, turned, packed)


def exchange_kernel(
    adv_hbm,
    imp_hbm,
    scale_hbm,
    class_hbm,
    elig_hbm,
    g_ref,
    aux_ref,
    adv_in,
    imp_in,
    scale_ref,
    class_ref,
    elig_ref,
    adv_buf,
    imp_buf,
    a_ref,
    column_ref,
    b_ref,
    e_ref,
    t_ref,
    p1_buf,
    p2_buf,
    wl_buf,
    quarter_buf,
    spend_buf,
    r1_ref,
    c2_ref,
    sums,
    rx_buf,
    rz_buf,
    w_ref,
    send_sem,
    recv_sem,
    in_sem,
):
    adv = lax.axis_index("adv")
    imp = lax.axis_index("imp")
    z = imp // NX
    x = lax.rem(imp, NX)

    def at_z(d):
        return lax.rem(z + (d + NZ), NZ)

    def at_x(e):
        return lax.rem(x + e, NX)

    def shard(d, e):
        return adv_buf.at[at_z(d), at_x(e)]

    partner = adv + 1 - 2 * lax.rem(adv, 2)

    def to_z(d):
        return (adv, at_z(d) * NX + x)

    def to_x(e):
        return (adv, z * NX + at_x(e))

    def to_adv(k):
        return (lax.rem(adv + k, NA), imp)

    def imps(e, whose, k):
        return imp_buf.at[at_x(NX - e), lax.rem(whose + (NA - 2 * k), NA)]

    started = []

    def remote(src, dst, number, device):
        return pltpu.make_async_remote_copy(
            src_ref=src,
            dst_ref=dst,
            send_sem=send_sem.at[number],
            recv_sem=recv_sem.at[number],
            device_id=device,
            device_id_type=MESH,
        )

    def send(src, dst, number, device):
        copy = remote(src, dst, number, device)
        copy.start()
        started.append(copy)

    def arrived(ref, number):
        remote(ref, ref, number, to_x(1)).wait_recv()

    loads = [
        pltpu.make_async_copy(src, dst, in_sem.at[n])
        for n, (src, dst) in enumerate(
            (
                (adv_hbm, adv_in),
                (imp_hbm, imp_in),
                (scale_hbm, scale_ref),
                (class_hbm, class_ref),
                (elig_hbm, elig_ref),
            )
        )
    ]
    for load in loads:
        load.start()

    barrier = pltpu.get_barrier_semaphore()
    peers = [to_z(d) for d in NEAR] + [to_x(e) for e in (1, 2, 3)] + [to_adv(k) for k in range(1, NA)]
    for device in peers:
        pl.semaphore_signal(barrier, inc=1, device_id=device, device_id_type=MESH)

    mine = shard(0, 0)
    loads[0].wait()
    adv_buf[z, x] = jnp.concatenate([adv_in[0:16, :], adv_in[16:32, :]], axis=1)
    loads[1].wait()
    imp_buf[x, adv] = jnp.concatenate([imp_in[0:32, :], imp_in[32:64, :]], axis=1)
    for load in loads[2:]:
        load.wait()
    allowance = 2.0 * jnp.exp(0.3 * class_ref[...].astype(F32) - 1.2)
    mask_rows = elig_ref[...].astype(F32)
    mask = mask_rows.T
    p1_buf[adv] = jnp.zeros((8, BLOCK), F32)
    for cb in range(4):
        p1_buf[adv, cb : cb + 1, :] = jnp.sum(allowance * mask[:, cb : cb + 1], axis=0, keepdims=True)

    pl.semaphore_wait(barrier, len(peers))

    for d in (4, -4, 3, -3, 2, -2, 1, -1):
        send(mine, mine, S_Z[-d], to_z(d))
    own = imps(0, adv, 0)
    for e in (2, 1, 3):
        send(own, own, S_IX[e], to_x(e))
    for k in (2, 1, 3):
        send(own, own, S_IY[0, k], to_adv(2 * k))
    send(own, own, S_IC[0, 0], (partner, imp))
    for k in range(1, NA):
        send(p1_buf.at[adv], p1_buf.at[adv], S_P1[k], to_adv(k))
    for e in (2, 1, 3):
        send(mine, mine, S_X[0, e], to_x(e))

    def pass_on(d):
        here = shard(d, 0)
        arrived(here, S_Z[d])
        if d == -4:
            for k in FAR_NEG:
                far = -4 - k
                send(here, here, S_Z[8 if far == -8 else far], to_z(k))
        if d == 4:
            for k in FAR_POS:
                send(here, here, S_Z[4 + k], to_z(-k))
        for e in (2, 1, 3):
            send(here, here, S_X[d, e], to_x(e))

    for d in (1, -1, 2, -2):
        pass_on(d)
    for e in (1, 3, 2):
        here = imps(e, adv, 0)
        arrived(here, S_IX[e])
        for k in (2, 1, 3):
            send(here, here, S_IY[e, k], to_adv(2 * k))
        send(here, here, S_IC[e, 0], (partner, imp))
    for d in (3, -3, 4, -4):
        pass_on(d)

    for k in range(1, NA):
        arrived(p1_buf.at[lax.rem(adv + (NA - k), NA)], S_P1[k])
    share = p1_buf[0]
    for k in range(1, NA):
        share = share + p1_buf[k]
    first_price = jnp.sum(share, axis=1, keepdims=True) / 32768.0
    weight_rows = mask_rows / first_price[0:4, :]
    place = lax.broadcasted_iota(jnp.int32, (4, BLOCK), 1) // 32
    for q in range(4):
        spread = jnp.zeros((4, BLOCK), F32)
        for k in range(4):
            spread = jnp.where(place == k, weight_rows[:, 4 * q + k : 4 * q + k + 1], spread)
        wl_buf[x, 4 * q : 4 * q + 4, :] = spread
    for e in (2, 1, 3):
        send(wl_buf.at[x], wl_buf.at[x], S_WX[e], to_x(e))
    for cb in range(4):
        w_ref[cb] = jnp.broadcast_to(mask[:, cb : cb + 1] / first_price[cb : cb + 1, :], (16, BLOCK))

    for e in (0, 1, 3, 2):
        for k in (1, 3, 2):
            here = imps(e, adv, k)
            arrived(here, S_IY[e, k])
            send(here, here, S_IC[e, k], (partner, imp))
    def prepare(xp):
        low_half, up_half = twice(imp_buf[xp] * (SCORE_GAIN * LOG2E))
        doubled = jnp.concatenate([low_half, up_half], axis=1).reshape(512, BLOCK)
        high, mid, low = split_parts(doubled)
        left = first_half((512, BLOCK))
        b_ref[xp, :, 0:128] = jnp.where(left, high, mid).astype(BF16)
        b_ref[xp, :, 128:256] = jnp.where(left, high, low).astype(BF16)
        b_ref[xp, :, 256:384] = jnp.where(left, mid, high).astype(BF16)

    def operand(shards):
        low_half, up_half = twice(shards)
        doubled = jnp.concatenate([low_half, up_half], axis=1).reshape(shards.shape[0] * 32, BLOCK)
        high, mid, low = split_parts(doubled)
        left = first_half(doubled.shape)
        return jnp.concatenate(
            [
                high.astype(BF16),
                jnp.where(left, mid, high).astype(BF16),
                jnp.where(left, mid, low).astype(BF16),
            ],
            axis=1,
        )

    def exp_scores(left_rows, right_rows):
        scores = lax.dot_general(
            left_rows, right_rows, (((1,), (1,)), ((), ())), preferred_element_type=F32
        )
        return jnp.exp2(scores)

    for e in (1, 3, 2):
        arrived(wl_buf.at[at_x(NX - e)], S_WX[e])
    for e in (0, 1, 3, 2):
        for k in range(4):
            arrived(imps(e, partner, k), S_IC[e, k])
        prepare(at_x(NX - e))
    for d in FAR_Z:
        pass_on(d)
    column_ref[...] = operand(adv_buf[:, x])
    totals = [jnp.zeros((8, BLOCK), F32) for _ in range(4)]
    for e in (0, 1, 3, 2):
        xp = at_x(NX - e)
        every = exp_scores(b_ref[xp], column_ref[...])
        for cb in range(4):
            values = jnp.sum(every[cb * BLOCK : cb * BLOCK + BLOCK].reshape(16, 8, 512), axis=0)
            for q in range(4):
                row = wl_buf[xp, 4 * q + cb : 4 * q + cb + 1, :]
                totals[q] = totals[q] + values[:, q * 128 : q * 128 + 128] * row
    for q in range(4):
        quarter_buf[z, q : q + 1, :] = jnp.sum(totals[q], axis=0, keepdims=True)

    for d in reversed(ALL_D[1:]):
        send(quarter_buf.at[z], quarter_buf.at[z], S_QZ[d], to_z(-d))

    for d in ALL_D:
        for e in (1, 2, 3):
            arrived(shard(d, NX - e), S_X[d, e])

    @pl.loop(0, 8)
    def _(p):
        rows = operand(adv_buf[pl.ds(p * 2, 2)].reshape(8, 16, BLOCK))
        a_ref[p] = rows
        for cb in range(4):
            e_ref[p, cb] = exp_scores(b_ref[x, cb * BLOCK : cb * BLOCK + BLOCK, :], rows)

    def tile_values(start, stop):
        @pl.loop(start, stop)
        def _(p):
            g_ref[pl.ds(pl.multiple_of(p * 256, 256), 256), :] = exp_scores(a_ref[p], b_ref[x])

    for d in ALL_D[1:]:
        arrived(quarter_buf.at[at_z(d)], S_QZ[d])
    spent = quarter_buf[0]
    for other in range(1, NZ):
        spent = spent + quarter_buf[other]

    for k in range(4):
        turned = pltpu.roll(spent, lax.rem(x - k + 4, 4) * 32, axis=1)
        turned = jnp.where(place == x, turned, 0.0)
        for q in range(4):
            spend_buf[x, 4 * q + k : 4 * q + k + 1, :] = turned[q : q + 1, :]
    for e in (2, 1, 3):
        send(spend_buf.at[x], spend_buf.at[x], S_QX[e], to_x(e))
    for e in (1, 3, 2):
        arrived(spend_buf.at[at_x(NX - e)], S_QX[e])

    scale = scale_ref[...]
    first_bid = allowance * scale / 32768.0
    spending = ((spend_buf[0] + spend_buf[1]) + (spend_buf[2] + spend_buf[3])) * first_bid
    pacing = allowance / jnp.maximum(spending, allowance)
    row_bid = first_bid * pacing
    for cb in range(4):
        r1_ref[cb] = row_bid * w_ref[cb]
    r1_ref[4] = row_bid

    mine_p2 = p2_buf.at[adv]
    p2_buf[adv] = jnp.ones((8, BLOCK), F32)
    for cb in range(4):
        total = None
        for rb in range(16):
            row = r1_ref[cb, rb : rb + 1, :]
            half = rb % 2
            term = e_ref[rb // 2, cb, :, half * 128 : half * 128 + 128] * row
            total = term if total is None else total + term
        p2_buf[adv, cb : cb + 1, :] = jnp.sum(total.T, axis=0, keepdims=True)

    for k in range(1, NA):
        send(mine_p2, mine_p2, S_P2[k], to_adv(k))

    @pl.loop(0, 8)
    def _(p):
        for half in range(2):
            for cb in range(4):
                row = r1_ref[cb, pl.ds(2 * p + half, 1), :]
                value = e_ref[p, cb, :, half * 128 : half * 128 + 128]
                e_ref[p, cb, :, half * 128 : half * 128 + 128] = (value * row) * value

    for k in range(1, NA):
        arrived(p2_buf.at[lax.rem(adv + (NA - k), NA)], S_P2[k])
    price = p2_buf[0]
    for k in range(1, NA):
        price = price + p2_buf[k]
    inverse = 1.0 / price
    for cb in range(4):
        c2_ref[cb] = jnp.broadcast_to(inverse[cb : cb + 1, :], (BLOCK, BLOCK)).T

    @pl.loop(0, 8)
    def _(p):
        for half in range(2):
            total = jnp.zeros((8, BLOCK), F32)
            for cb in range(4):
                gain = e_ref[p, cb, :, half * 128 : half * 128 + 128] * c2_ref[cb]
                total = total + jnp.sum(gain.reshape(16, 8, BLOCK), axis=0)
            t_ref[pl.ds(2 * p + half, 1), :] = jnp.sum(total, axis=0, keepdims=True)

    def tile_gains(start, stop):
        @pl.loop(start, stop)
        def _(p):
            for half in range(2):
                rb = 2 * p + half
                rows = pl.ds(pl.multiple_of(p * 256 + half * 128, 128), 128)
                first = jnp.broadcast_to(r1_ref[4, pl.ds(rb, 1), :], (BLOCK, BLOCK)).T
                for cb in range(4):
                    value = g_ref[rows, cb * 128 : cb * 128 + 128]
                    bid = value * (first * w_ref[cb, pl.ds(rb, 1), :])
                    g_ref[rows, cb * 128 : cb * 128 + 128] = bid * inverse[cb : cb + 1, :] * value

    part = t_ref[...]
    sums[0] = part
    for e in (2, 1, 3):
        send(sums.at[0], rx_buf.at[e - 1], S_RX[e], to_x(e))
    tile_values(0, 8)
    for e in (1, 3, 2):
        arrived(rx_buf.at[e - 1], S_RX[e])
    total = part + rx_buf[1] + (rx_buf[0] + rx_buf[2])
    sums[1] = total
    index = {d: i for i, d in enumerate(WINDOW + JUMP + (8,))}
    for d in (2, -2, 1, -1, 8):
        send(sums.at[1], rz_buf.at[index[d]], S_RZ[d], to_z(-d))
    tile_gains(0, 4)
    for d in WINDOW:
        arrived(rz_buf.at[index[d]], S_RZ[d])
    window = total + ((rz_buf[0] + rz_buf[1]) + (rz_buf[2] + rz_buf[3]))
    sums[2] = window
    for d in JUMP:
        send(sums.at[2], rz_buf.at[index[d]], S_RZ[d], to_z(-d))
    tile_gains(4, 8)
    for copy in started:
        copy.wait_send()
    for d in JUMP + (8,):
        arrived(rz_buf.at[index[d]], S_RZ[d])
    spending = (window + (rz_buf[4] + rz_buf[5]) + rz_buf[6]) * scale
    pacing = allowance / jnp.maximum(spending, allowance)
    aux_ref[0:16] = scale * pacing * 16384.0
    aux_ref[16:32] = pacing
    aux_ref[32:40] = price


def scale_kernel(g_ref, aux_ref, out_hbm, price_hbm, pacing_hbm, out_ref, sem):
    small = [
        pltpu.make_async_copy(aux_ref.at[32:36], price_hbm, sem.at[8]),
        pltpu.make_async_copy(aux_ref.at[16:32], pacing_hbm, sem.at[9]),
    ]
    copies = []
    for p in range(8):
        for half in range(2):
            rb = 2 * p + half
            column = jnp.broadcast_to(aux_ref[rb : rb + 1, :], (BLOCK, BLOCK)).T
            rows = slice(rb * 128, rb * 128 + 128)
            for cb in range(4):
                columns = slice(cb * 128, cb * 128 + 128)
                out_ref[rows, columns] = g_ref[rows, columns] * column
        span = slice(p * 256, p * 256 + 256)
        copies.append(pltpu.make_async_copy(out_ref.at[span], out_hbm.at[span], sem.at[p]))
        copies[-1].start()
    for copy in small:
        copy.start()
    for copy in copies + small:
        copy.wait()


def per_device(adv_embed, imp_embed, value_scale, spend_class, eligible):
    hbm = pl.BlockSpec(memory_space=pltpu.HBM)
    vmem = pl.BlockSpec(memory_space=pltpu.VMEM)
    gains, aux = pl.pallas_call(
        exchange_kernel,
        out_shape=(
            jax.ShapeDtypeStruct((2048, 512), F32),
            jax.ShapeDtypeStruct((40, BLOCK), F32),
        ),
        in_specs=[hbm] * 5,
        out_specs=[vmem] * 2,
        scratch_shapes=[
            pltpu.VMEM((32, 64), F32),
            pltpu.VMEM((64, 64), F32),
            pltpu.VMEM((16, BLOCK), F32),
            pltpu.VMEM((16, BLOCK), jnp.int32),
            pltpu.VMEM((4, 16), jnp.int32),
            pltpu.VMEM((NZ, NX, 16, BLOCK), F32),
            pltpu.VMEM((NX, NA, 32, BLOCK), F32),
            pltpu.VMEM((8, 256, 384), BF16),
            pltpu.VMEM((512, 384), BF16),
            pltpu.VMEM((NX, 512, 384), BF16),
            pltpu.VMEM((8, 4, BLOCK, 256), F32),
            pltpu.VMEM((16, BLOCK), F32),
            pltpu.VMEM((NA, 8, BLOCK), F32),
            pltpu.VMEM((NA, 8, BLOCK), F32),
            pltpu.VMEM((NX, 16, BLOCK), F32),
            pltpu.VMEM((NZ, 4, BLOCK), F32),
            pltpu.VMEM((NX, 16, BLOCK), F32),
            pltpu.VMEM((5, 16, BLOCK), F32),
            pltpu.VMEM((4, BLOCK, BLOCK), F32),
            pltpu.VMEM((3, 16, BLOCK), F32),
            pltpu.VMEM((3, 16, BLOCK), F32),
            pltpu.VMEM((7, 16, BLOCK), F32),
            pltpu.VMEM((4, 16, BLOCK), F32),
            pltpu.SemaphoreType.DMA((N_SEM,)),
            pltpu.SemaphoreType.DMA((N_SEM,)),
            pltpu.SemaphoreType.DMA((5,)),
        ],
        compiler_params=pltpu.CompilerParams(
            collective_id=0, has_side_effects=True, vmem_limit_bytes=32 * 1024 * 1024
        ),
        name="exchange",
    )(
        *(
            pltpu.with_memory_space_constraint(operand, pltpu.HBM)
            for operand in (
                adv_embed,
                imp_embed,
                value_scale.reshape(16, BLOCK),
                spend_class.reshape(16, BLOCK),
                eligible.T,
            )
        )
    )
    density, prices, pacing = pl.pallas_call(
        scale_kernel,
        out_shape=(
            jax.ShapeDtypeStruct((2048, 512), F32),
            jax.ShapeDtypeStruct((4, BLOCK), F32),
            jax.ShapeDtypeStruct((16, BLOCK), F32),
        ),
        in_specs=[vmem] * 2,
        out_specs=[hbm] * 3,
        scratch_shapes=[
            pltpu.VMEM((2048, 512), F32),
            pltpu.SemaphoreType.DMA((10,)),
        ],
        compiler_params=pltpu.CompilerParams(vmem_limit_bytes=32 * 1024 * 1024),
        name="scale",
    )(gains, aux)
    return density, prices.reshape(512), pacing.reshape(2048)


def solution(mesh):
    in_specs = (
        P(("adv", "imp"), None),
        P(("imp", "adv"), None),
        P("adv"),
        P("adv"),
        P("adv", "imp"),
    )
    out_specs = (P("adv", "imp"), P("imp"), P("adv"))
    return jax.shard_map(
        per_device, mesh=mesh, in_specs=in_specs, out_specs=out_specs, check_vma=False
    )
```

```python
import functools

import jax
import jax.numpy as jnp
from jax import lax
from jax.experimental import pallas as pl
from jax.experimental.pallas import tpu as pltpu
from jax.sharding import PartitionSpec as P

MESH = pl.DeviceIdType.MESH
BLOCK = 128
SCORE_GAIN = 0.0875
LOG2E = 1.4426950408889634
NX = 4
NZ = 16
NA = 8
F32 = jnp.float32
BF16 = jnp.bfloat16

FAR_Z = (5, -5, 6, -6, 7, -7, 8)
NEAR = (1, -1, 2, -2, 3, -3, 4, -4)
FAR_NEG = (1, 2, 3, 4)
FAR_POS = (1, 2, 3)
WINDOW = (1, -1, 2, -2)
JUMP = (5, -5)
ALL_D = (0, 1, -1, 2, -2, 3, -3, 4, -4, 5, -5, 6, -6, 7, -7, 8)

_n = 0
S_Z = {}
for _d in ALL_D[1:]:
    S_Z[_d] = _n
    _n += 1
S_X = {}
for _d in ALL_D:
    for _e in (1, 2, 3):
        S_X[_d, _e] = _n
        _n += 1
S_P1 = {}
S_P2 = {}
for _k in range(1, NA):
    S_P1[_k] = _n
    S_P2[_k] = _n + 1
    _n += 2
S_IX = {}
S_WX = {}
S_QX = {}
S_RX = {}
for _e in (1, 2, 3):
    S_IX[_e] = _n
    S_WX[_e] = _n + 1
    S_QX[_e] = _n + 2
    S_RX[_e] = _n + 3
    _n += 4
S_IY = {}
S_IC = {}
for _e in range(4):
    for _k in range(4):
        if _k:
            S_IY[_e, _k] = _n
            _n += 1
        S_IC[_e, _k] = _n
        _n += 1
S_QZ = {}
for _d in ALL_D[1:]:
    S_QZ[_d] = _n
    _n += 1
S_RZ = {}
for _d in WINDOW + JUMP + (8,):
    S_RZ[_d] = _n
    _n += 1
N_SEM = _n


def split_parts(rows):
    high = rows.astype(BF16).astype(F32)
    rest = rows - high
    mid = rest.astype(BF16).astype(F32)
    low = rest - mid
    return high, mid, low


def first_half(shape):
    return lax.broadcasted_iota(jnp.int32, shape, len(shape) - 1) < 64


def twice(packed):
    turned = pltpu.roll(packed, 64, axis=len(packed.shape) - 1)
    left = first_half(packed.shape)
    return jnp.where(left, packed, turned), jnp.where(left, turned, packed)


def exchange_kernel(
    adv_hbm,
    imp_hbm,
    scale_hbm,
    class_hbm,
    elig_hbm,
    g_ref,
    aux_ref,
    adv_in,
    imp_in,
    scale_ref,
    class_ref,
    elig_ref,
    adv_buf,
    imp_buf,
    a_ref,
    column_ref,
    b_ref,
    e_ref,
    t_ref,
    p1_buf,
    p2_buf,
    wl_buf,
    quarter_buf,
    spend_buf,
    r1_ref,
    c2_ref,
    sums,
    rx_buf,
    rz_buf,
    w_ref,
    send_sem,
    recv_sem,
    in_sem,
):
    adv = lax.axis_index("adv")
    imp = lax.axis_index("imp")
    z = imp // NX
    x = lax.rem(imp, NX)

    def at_z(d):
        return lax.rem(z + (d + NZ), NZ)

    def at_x(e):
        return lax.rem(x + e, NX)

    def shard(d, e):
        return adv_buf.at[at_z(d), at_x(e)]

    partner = adv + 1 - 2 * lax.rem(adv, 2)

    def to_z(d):
        return (adv, at_z(d) * NX + x)

    def to_x(e):
        return (adv, z * NX + at_x(e))

    def to_adv(k):
        return (lax.rem(adv + k, NA), imp)

    def imps(e, whose, k):
        return imp_buf.at[at_x(NX - e), lax.rem(whose + (NA - 2 * k), NA)]

    started = []

    def remote(src, dst, number, device):
        return pltpu.make_async_remote_copy(
            src_ref=src,
            dst_ref=dst,
            send_sem=send_sem.at[number],
            recv_sem=recv_sem.at[number],
            device_id=device,
            device_id_type=MESH,
        )

    def send(src, dst, number, device):
        copy = remote(src, dst, number, device)
        copy.start()
        started.append(copy)

    def arrived(ref, number):
        remote(ref, ref, number, to_x(1)).wait_recv()

    loads = [
        pltpu.make_async_copy(src, dst, in_sem.at[n])
        for n, (src, dst) in enumerate(
            (
                (adv_hbm, adv_in),
                (imp_hbm, imp_in),
                (scale_hbm, scale_ref),
                (class_hbm, class_ref),
                (elig_hbm, elig_ref),
            )
        )
    ]
    for load in loads:
        load.start()

    barrier = pltpu.get_barrier_semaphore()
    peers = [to_z(d) for d in reversed(NEAR)] + [to_x(e) for e in (1, 2, 3)] + [to_adv(k) for k in range(1, NA)]
    for device in peers:
        pl.semaphore_signal(barrier, inc=1, device_id=device, device_id_type=MESH)

    mine = shard(0, 0)
    loads[0].wait()
    adv_buf[z, x] = jnp.concatenate([adv_in[0:16, :], adv_in[16:32, :]], axis=1)
    loads[1].wait()
    imp_buf[x, adv] = jnp.concatenate([imp_in[0:32, :], imp_in[32:64, :]], axis=1)
    pl.semaphore_wait(barrier, len(peers))

    for d in (4, -4, 3, -3, 2, -2, 1, -1):
        send(mine, mine, S_Z[-d], to_z(d))
    own = imps(0, adv, 0)
    for e in (2, 1, 3):
        send(own, own, S_IX[e], to_x(e))
    for k in (2, 1, 3):
        send(own, own, S_IY[0, k], to_adv(2 * k))
    send(own, own, S_IC[0, 0], (partner, imp))
    for load in loads[2:]:
        load.wait()
    allowance = 2.0 * jnp.exp(0.3 * class_ref[...].astype(F32) - 1.2)
    mask_rows = elig_ref[...].astype(F32)
    mask = mask_rows.T
    p1_buf[adv] = jnp.zeros((8, BLOCK), F32)
    for cb in range(4):
        p1_buf[adv, cb : cb + 1, :] = jnp.sum(allowance * mask[:, cb : cb + 1], axis=0, keepdims=True)
    for k in range(1, NA):
        send(p1_buf.at[adv], p1_buf.at[adv], S_P1[k], to_adv(k))
    for e in (2, 1, 3):
        send(mine, mine, S_X[0, e], to_x(e))

    def pass_on(d):
        here = shard(d, 0)
        arrived(here, S_Z[d])
        if d == -4:
            for k in FAR_NEG:
                far = -4 - k
                send(here, here, S_Z[8 if far == -8 else far], to_z(k))
        if d == 4:
            for k in FAR_POS:
                send(here, here, S_Z[4 + k], to_z(-k))
        for e in (2, 1, 3):
            send(here, here, S_X[d, e], to_x(e))

    for d in (1, -1, 2, -2):
        pass_on(d)
    for e in (1, 3, 2):
        here = imps(e, adv, 0)
        arrived(here, S_IX[e])
        for k in (2, 1, 3):
            send(here, here, S_IY[e, k], to_adv(2 * k))
        send(here, here, S_IC[e, 0], (partner, imp))
    for d in (3, -3, 4, -4):
        pass_on(d)

    for k in range(1, NA):
        arrived(p1_buf.at[lax.rem(adv + (NA - k), NA)], S_P1[k])
    share = p1_buf[0]
    for k in range(1, NA):
        share = share + p1_buf[k]
    first_price = jnp.sum(share, axis=1, keepdims=True) / 32768.0
    weight_rows = mask_rows / first_price[0:4, :]
    place = lax.broadcasted_iota(jnp.int32, (4, BLOCK), 1) // 32
    for q in range(4):
        spread = jnp.zeros((4, BLOCK), F32)
        for k in range(4):
            spread = jnp.where(place == k, weight_rows[:, 4 * q + k : 4 * q + k + 1], spread)
        wl_buf[x, 4 * q : 4 * q + 4, :] = spread
    for e in (2, 1, 3):
        send(wl_buf.at[x], wl_buf.at[x], S_WX[e], to_x(e))
    for cb in range(4):
        w_ref[cb] = jnp.broadcast_to(mask[:, cb : cb + 1] / first_price[cb : cb + 1, :], (16, BLOCK))

    for e in (0, 1, 3, 2):
        for k in (1, 3, 2):
            here = imps(e, adv, k)
            arrived(here, S_IY[e, k])
            send(here, here, S_IC[e, k], (partner, imp))
    def prepare(xp):
        low_half, up_half = twice(imp_buf[xp] * (SCORE_GAIN * LOG2E))
        doubled = jnp.concatenate([low_half, up_half], axis=1).reshape(512, BLOCK)
        high, mid, low = split_parts(doubled)
        left = first_half((512, BLOCK))
        b_ref[xp, :, 0:128] = jnp.where(left, high, mid).astype(BF16)
        b_ref[xp, :, 128:256] = jnp.where(left, high, low).astype(BF16)
        b_ref[xp, :, 256:384] = jnp.where(left, mid, high).astype(BF16)

    def operand(shards):
        low_half, up_half = twice(shards)
        doubled = jnp.concatenate([low_half, up_half], axis=1).reshape(shards.shape[0] * 32, BLOCK)
        high, mid, low = split_parts(doubled)
        left = first_half(doubled.shape)
        return jnp.concatenate(
            [
                high.astype(BF16),
                jnp.where(left, mid, high).astype(BF16),
                jnp.where(left, mid, low).astype(BF16),
            ],
            axis=1,
        )

    def exp_scores(left_rows, right_rows):
        scores = lax.dot_general(
            left_rows, right_rows, (((1,), (1,)), ((), ())), preferred_element_type=F32
        )
        return jnp.exp2(scores)

    for e in (1, 3, 2):
        arrived(wl_buf.at[at_x(NX - e)], S_WX[e])
    for e in (0, 1, 3, 2):
        for k in range(4):
            arrived(imps(e, partner, k), S_IC[e, k])
        prepare(at_x(NX - e))
    for d in FAR_Z:
        pass_on(d)
    column_ref[...] = operand(adv_buf[:, x])
    totals = [jnp.zeros((8, BLOCK), F32) for _ in range(4)]
    for e in (0, 1, 3, 2):
        xp = at_x(NX - e)
        every = exp_scores(b_ref[xp], column_ref[...])
        for cb in range(4):
            values = jnp.sum(every[cb * BLOCK : cb * BLOCK + BLOCK].reshape(16, 8, 512), axis=0)
            for q in range(4):
                row = wl_buf[xp, 4 * q + cb : 4 * q + cb + 1, :]
                totals[q] = totals[q] + values[:, q * 128 : q * 128 + 128] * row
    for q in range(4):
        quarter_buf[z, q : q + 1, :] = jnp.sum(totals[q], axis=0, keepdims=True)

    for d in reversed(ALL_D[1:]):
        send(quarter_buf.at[z], quarter_buf.at[z], S_QZ[d], to_z(-d))

    for d in ALL_D:
        for e in (1, 2, 3):
            arrived(shard(d, NX - e), S_X[d, e])

    @pl.loop(0, 8)
    def _(p):
        rows = operand(adv_buf[pl.ds(p * 2, 2)].reshape(8, 16, BLOCK))
        a_ref[p] = rows
        for cb in range(4):
            e_ref[p, cb] = exp_scores(b_ref[x, cb * BLOCK : cb * BLOCK + BLOCK, :], rows)

    def tile_values(start, stop):
        @pl.loop(start, stop)
        def _(p):
            g_ref[pl.ds(pl.multiple_of(p * 256, 256), 256), :] = exp_scores(a_ref[p], b_ref[x])

    for d in ALL_D[1:]:
        arrived(quarter_buf.at[at_z(d)], S_QZ[d])
    spent = quarter_buf[0]
    for other in range(1, NZ):
        spent = spent + quarter_buf[other]

    for k in range(4):
        turned = pltpu.roll(spent, lax.rem(x - k + 4, 4) * 32, axis=1)
        turned = jnp.where(place == x, turned, 0.0)
        for q in range(4):
            spend_buf[x, 4 * q + k : 4 * q + k + 1, :] = turned[q : q + 1, :]
    for e in (2, 1, 3):
        send(spend_buf.at[x], spend_buf.at[x], S_QX[e], to_x(e))
    for e in (1, 3, 2):
        arrived(spend_buf.at[at_x(NX - e)], S_QX[e])

    scale = scale_ref[...]
    first_bid = allowance * scale / 32768.0
    spending = ((spend_buf[0] + spend_buf[1]) + (spend_buf[2] + spend_buf[3])) * first_bid
    pacing = allowance / jnp.maximum(spending, allowance)
    row_bid = first_bid * pacing
    for cb in range(4):
        r1_ref[cb] = row_bid * w_ref[cb]
    r1_ref[4] = row_bid

    mine_p2 = p2_buf.at[adv]
    p2_buf[adv] = jnp.ones((8, BLOCK), F32)
    for cb in range(4):
        total = None
        for rb in range(16):
            row = r1_ref[cb, rb : rb + 1, :]
            half = rb % 2
            term = e_ref[rb // 2, cb, :, half * 128 : half * 128 + 128] * row
            total = term if total is None else total + term
        p2_buf[adv, cb : cb + 1, :] = jnp.sum(total.T, axis=0, keepdims=True)

    for k in range(1, NA):
        send(mine_p2, mine_p2, S_P2[k], to_adv(k))

    @pl.loop(0, 8)
    def _(p):
        for half in range(2):
            for cb in range(4):
                row = r1_ref[cb, pl.ds(2 * p + half, 1), :]
                value = e_ref[p, cb, :, half * 128 : half * 128 + 128]
                e_ref[p, cb, :, half * 128 : half * 128 + 128] = (value * row) * value

    for k in range(1, NA):
        arrived(p2_buf.at[lax.rem(adv + (NA - k), NA)], S_P2[k])
    price = p2_buf[0]
    for k in range(1, NA):
        price = price + p2_buf[k]
    inverse = 1.0 / price
    for cb in range(4):
        c2_ref[cb] = jnp.broadcast_to(inverse[cb : cb + 1, :], (BLOCK, BLOCK)).T

    @pl.loop(0, 8)
    def _(p):
        for half in range(2):
            total = jnp.zeros((8, BLOCK), F32)
            for cb in range(4):
                gain = e_ref[p, cb, :, half * 128 : half * 128 + 128] * c2_ref[cb]
                total = total + jnp.sum(gain.reshape(16, 8, BLOCK), axis=0)
            t_ref[pl.ds(2 * p + half, 1), :] = jnp.sum(total, axis=0, keepdims=True)

    def tile_gains(start, stop):
        @pl.loop(start, stop)
        def _(p):
            for half in range(2):
                rb = 2 * p + half
                rows = pl.ds(pl.multiple_of(p * 256 + half * 128, 128), 128)
                first = jnp.broadcast_to(r1_ref[4, pl.ds(rb, 1), :], (BLOCK, BLOCK)).T
                for cb in range(4):
                    value = g_ref[rows, cb * 128 : cb * 128 + 128]
                    bid = value * (first * w_ref[cb, pl.ds(rb, 1), :])
                    g_ref[rows, cb * 128 : cb * 128 + 128] = bid * inverse[cb : cb + 1, :] * value

    part = t_ref[...]
    sums[0] = part
    for e in (2, 1, 3):
        send(sums.at[0], rx_buf.at[e - 1], S_RX[e], to_x(e))
    tile_values(0, 8)
    for e in (1, 3, 2):
        arrived(rx_buf.at[e - 1], S_RX[e])
    total = part + rx_buf[1] + (rx_buf[0] + rx_buf[2])
    sums[1] = total
    index = {d: i for i, d in enumerate(WINDOW + JUMP + (8,))}
    for d in (2, -2, 1, -1, 8):
        send(sums.at[1], rz_buf.at[index[d]], S_RZ[d], to_z(-d))
    tile_gains(0, 4)
    for d in WINDOW:
        arrived(rz_buf.at[index[d]], S_RZ[d])
    window = total + ((rz_buf[0] + rz_buf[1]) + (rz_buf[2] + rz_buf[3]))
    sums[2] = window
    for d in JUMP:
        send(sums.at[2], rz_buf.at[index[d]], S_RZ[d], to_z(-d))
    tile_gains(4, 8)
    for copy in started:
        copy.wait_send()
    for d in JUMP + (8,):
        arrived(rz_buf.at[index[d]], S_RZ[d])
    spending = (window + (rz_buf[4] + rz_buf[5]) + rz_buf[6]) * scale
    pacing = allowance / jnp.maximum(spending, allowance)
    aux_ref[0:16] = scale * pacing * 16384.0
    aux_ref[16:32] = pacing
    aux_ref[32:40] = price


def scale_kernel(g_ref, aux_ref, out_hbm, price_hbm, pacing_hbm, out_ref, sem):
    small = [
        pltpu.make_async_copy(aux_ref.at[32:36], price_hbm, sem.at[8]),
        pltpu.make_async_copy(aux_ref.at[16:32], pacing_hbm, sem.at[9]),
    ]
    copies = []
    for p in range(8):
        for half in range(2):
            rb = 2 * p + half
            column = jnp.broadcast_to(aux_ref[rb : rb + 1, :], (BLOCK, BLOCK)).T
            rows = slice(rb * 128, rb * 128 + 128)
            for cb in range(4):
                columns = slice(cb * 128, cb * 128 + 128)
                out_ref[rows, columns] = g_ref[rows, columns] * column
        span = slice(p * 256, p * 256 + 256)
        copies.append(pltpu.make_async_copy(out_ref.at[span], out_hbm.at[span], sem.at[p]))
        copies[-1].start()
    for copy in small:
        copy.start()
    for copy in copies + small:
        copy.wait()


def per_device(adv_embed, imp_embed, value_scale, spend_class, eligible):
    hbm = pl.BlockSpec(memory_space=pltpu.HBM)
    vmem = pl.BlockSpec(memory_space=pltpu.VMEM)
    gains, aux = pl.pallas_call(
        exchange_kernel,
        out_shape=(
            jax.ShapeDtypeStruct((2048, 512), F32),
            jax.ShapeDtypeStruct((40, BLOCK), F32),
        ),
        in_specs=[hbm] * 5,
        out_specs=[vmem] * 2,
        scratch_shapes=[
            pltpu.VMEM((32, 64), F32),
            pltpu.VMEM((64, 64), F32),
            pltpu.VMEM((16, BLOCK), F32),
            pltpu.VMEM((16, BLOCK), jnp.int32),
            pltpu.VMEM((4, 16), jnp.int32),
            pltpu.VMEM((NZ, NX, 16, BLOCK), F32),
            pltpu.VMEM((NX, NA, 32, BLOCK), F32),
            pltpu.VMEM((8, 256, 384), BF16),
            pltpu.VMEM((512, 384), BF16),
            pltpu.VMEM((NX, 512, 384), BF16),
            pltpu.VMEM((8, 4, BLOCK, 256), F32),
            pltpu.VMEM((16, BLOCK), F32),
            pltpu.VMEM((NA, 8, BLOCK), F32),
            pltpu.VMEM((NA, 8, BLOCK), F32),
            pltpu.VMEM((NX, 16, BLOCK), F32),
            pltpu.VMEM((NZ, 4, BLOCK), F32),
            pltpu.VMEM((NX, 16, BLOCK), F32),
            pltpu.VMEM((5, 16, BLOCK), F32),
            pltpu.VMEM((4, BLOCK, BLOCK), F32),
            pltpu.VMEM((3, 16, BLOCK), F32),
            pltpu.VMEM((3, 16, BLOCK), F32),
            pltpu.VMEM((7, 16, BLOCK), F32),
            pltpu.VMEM((4, 16, BLOCK), F32),
            pltpu.SemaphoreType.DMA((N_SEM,)),
            pltpu.SemaphoreType.DMA((N_SEM,)),
            pltpu.SemaphoreType.DMA((5,)),
        ],
        compiler_params=pltpu.CompilerParams(
            collective_id=0, has_side_effects=True, vmem_limit_bytes=32 * 1024 * 1024
        ),
        name="exchange",
    )(
        *(
            pltpu.with_memory_space_constraint(operand, pltpu.HBM)
            for operand in (
                adv_embed,
                imp_embed,
                value_scale.reshape(16, BLOCK),
                spend_class.reshape(16, BLOCK),
                eligible.T,
            )
        )
    )
    density, prices, pacing = pl.pallas_call(
        scale_kernel,
        out_shape=(
            jax.ShapeDtypeStruct((2048, 512), F32),
            jax.ShapeDtypeStruct((4, BLOCK), F32),
            jax.ShapeDtypeStruct((16, BLOCK), F32),
        ),
        in_specs=[vmem] * 2,
        out_specs=[hbm] * 3,
        scratch_shapes=[
            pltpu.VMEM((2048, 512), F32),
            pltpu.SemaphoreType.DMA((10,)),
        ],
        compiler_params=pltpu.CompilerParams(vmem_limit_bytes=32 * 1024 * 1024),
        name="scale",
    )(gains, aux)
    return density, prices.reshape(512), pacing.reshape(2048)


def solution(mesh):
    in_specs = (
        P(("adv", "imp"), None),
        P(("imp", "adv"), None),
        P("adv"),
        P("adv"),
        P("adv", "imp"),
    )
    out_specs = (P("adv", "imp"), P("imp"), P("adv"))
    return jax.shard_map(
        per_device, mesh=mesh, in_specs=in_specs, out_specs=out_specs, check_vma=False
    )
```
